512 devices in a mesh: ctx: 64 (over z, x_lo, core), tp: 8 (over x_hi, y).
Axes of the slice: x: 4 (x_hi: 2, x_lo: 2; x = x_hi * 2 + x_lo), y: 4, z: 16, core: 2. Of those that a mesh axis runs over, the one named last changes fastest.
Arguments:
- query: bfloat16 [8192, 4096], P(('ctx', 'tp')), may hold values from -200 to 200
- keys: bfloat16 [8192, 1024], P(('ctx', 'tp')), may hold values from -20 to 20
- values: bfloat16 [8192, 1024], P(('ctx', 'tp')), may hold values from -6 to 6
- output_gradient: bfloat16 [8192, 4096], P(('ctx', 'tp')), may hold values from -6 to 6
Outputs:
- attn_out: bfloat16 [8192, 4096], P(('ctx', 'tp'))
- grad_query: bfloat16 [8192, 4096], P(('ctx', 'tp'))
- key_gradient: bfloat16 [8192, 1024], P(('ctx', 'tp'))
- value_gradient: bfloat16 [8192, 1024], P(('ctx', 'tp'))
The draws below stay inside these ranges and needn't reach their ends.
All inputs are finite; a program needn't handle non-finite values.
Results may differ from the reference program's by a relative error of at most 0.025.
Values may be sent and summed in bfloat16 or wider, within the bound.
No kernel may reach another device: no remote copies, remote signals or barrier semaphores. Data moves between devices by JAX's collectives and lax.ppermute only.
A program may use at most 64 MiB of HBM per device.

```python
import jax
import jax.numpy as jnp
from jax import lax

HEAD_WIDTH = 128
KEY_VALUE_HEADS = 8
QUERY_GROUP = 4
HQ = 32
TOKEN_COUNT = 8192


def draw_pair(key):
    key_offset = jax.random.truncated_normal(jax.random.fold_in(key, 11), -5.0, 5.0, (TOKEN_COUNT, KEY_VALUE_HEADS, HEAD_WIDTH), jnp.float32)
    query_offset = jax.random.truncated_normal(jax.random.fold_in(key, 12), -5.0, 5.0, (TOKEN_COUNT, KEY_VALUE_HEADS, QUERY_GROUP, HEAD_WIDTH), jnp.float32)
    key_row_block = key_offset
    query_row_block = query_offset
    return (query_row_block.reshape(TOKEN_COUNT, KEY_VALUE_HEADS * QUERY_GROUP * HEAD_WIDTH), key_row_block.reshape(TOKEN_COUNT, KEY_VALUE_HEADS * HEAD_WIDTH))


def draw_query(key, part):
    return draw_pair(key)[0].astype(jnp.bfloat16)


def draw_keys(key, part):
    return draw_pair(key)[1].astype(jnp.bfloat16)


def levels(key, dims, pieces, smallest, top_value):
    loudness, own = 1.0, jax.random.fold_in(key, 6)
    for dim, blocks in pieces:
        draws = jnp.exp(jax.random.uniform(jax.random.fold_in(own, dim), (blocks,), jnp.float32, smallest / len(pieces), top_value / len(pieces)))
        loudness = loudness * jnp.repeat(draws, dims[dim] // blocks).reshape([-1 if axis == dim else 1 for axis in range(len(dims))])
    return loudness


def scatter_about(own_key, extent, width, limit, shards=(), held_as=jnp.bfloat16):
    factor_of = levels(own_key, extent, shards, -0.22, 0.18) if shards else 1.0
    drawn = jax.random.normal(own_key, extent, jnp.float32) * width * factor_of
    return jnp.minimum(jnp.maximum(drawn, -limit), limit).astype(held_as)


def setup_inputs(seed: int = 0) -> dict:
    streams_of = jax.random.split(jax.random.key(seed), 5)
    return {
        "query": draw_query(jax.random.fold_in(streams_of[4], 71), 0),
        "keys": draw_keys(jax.random.fold_in(streams_of[4], 71), 0),
        "values": scatter_about(streams_of[2], (TOKEN_COUNT, KEY_VALUE_HEADS * HEAD_WIDTH), 1.0, 6.0, ((0, 512),)),
        "output_gradient": scatter_about(streams_of[3], (TOKEN_COUNT, HQ * HEAD_WIDTH), 1.0, 6.0, ((0, 512),)),
    }


def one_group(group_args):
    group_query, group_keys, group_values, group_grad = group_args
    score_scale = HEAD_WIDTH ** -0.5
    position = jnp.arange(TOKEN_COUNT)
    allowed = position[:, None] >= position[None, :]
    key_sum = jnp.zeros((TOKEN_COUNT, HEAD_WIDTH), jnp.float32)
    value_sum = jnp.zeros((TOKEN_COUNT, HEAD_WIDTH), jnp.float32)
    outputs = []
    query_grads = []
    for head in range(QUERY_GROUP):
        head_query = group_query[:, head]
        head_grad = group_grad[:, head]
        logits = score_scale * jnp.dot(head_query, group_keys.T, preferred_element_type=jnp.float32)
        logits = jnp.where(allowed, logits, -1e30)
        row_max = jnp.max(logits, axis=1, keepdims=True)
        lse = row_max + jnp.log(jnp.sum(jnp.exp(logits - row_max), axis=1, keepdims=True))
        probs = jnp.where(allowed, jnp.exp(logits - lse), 0.0)
        weights = probs.astype(jnp.bfloat16)
        attention = jnp.dot(weights, group_values, preferred_element_type=jnp.float32).astype(jnp.bfloat16)
        row_delta = jnp.sum(head_grad.astype(jnp.float32) * attention.astype(jnp.float32), axis=1, keepdims=True)
        prob_grad = jnp.dot(head_grad, group_values.T, preferred_element_type=jnp.float32)
        score_grad = (probs * (prob_grad - row_delta)).astype(jnp.bfloat16)
        query_grads.append((score_scale * jnp.dot(score_grad, group_keys, preferred_element_type=jnp.float32)).astype(jnp.bfloat16))
        outputs.append(attention)
        key_sum = key_sum + jnp.dot(score_grad.T, head_query, preferred_element_type=jnp.float32)
        value_sum = value_sum + jnp.dot(weights.T, head_grad, preferred_element_type=jnp.float32)
    return (jnp.stack(outputs, axis=1), jnp.stack(query_grads, axis=1),
            (score_scale * key_sum).astype(jnp.bfloat16), value_sum.astype(jnp.bfloat16))


def reference(query, keys, values, output_gradient):
    query_grouped = query.reshape(TOKEN_COUNT, KEY_VALUE_HEADS, QUERY_GROUP, HEAD_WIDTH).transpose(1, 0, 2, 3)
    gradient_grouped = output_gradient.reshape(TOKEN_COUNT, KEY_VALUE_HEADS, QUERY_GROUP, HEAD_WIDTH).transpose(1, 0, 2, 3)
    keys_grouped = keys.reshape(TOKEN_COUNT, KEY_VALUE_HEADS, HEAD_WIDTH).transpose(1, 0, 2)
    values_grouped = values.reshape(TOKEN_COUNT, KEY_VALUE_HEADS, HEAD_WIDTH).transpose(1, 0, 2)
    attention, query_grad, key_gradient_rows, value_gradient_rows = lax.map(one_group, (query_grouped, keys_grouped, values_grouped, gradient_grouped))
    attn_out = attention.transpose(1, 0, 2, 3).reshape(TOKEN_COUNT, HQ * HEAD_WIDTH)
    grad_query = query_grad.transpose(1, 0, 2, 3).reshape(TOKEN_COUNT, HQ * HEAD_WIDTH)
    key_gradient = key_gradient_rows.transpose(1, 0, 2).reshape(TOKEN_COUNT, KEY_VALUE_HEADS * HEAD_WIDTH)
    value_gradient = value_gradient_rows.transpose(1, 0, 2).reshape(TOKEN_COUNT, KEY_VALUE_HEADS * HEAD_WIDTH)
    return (attn_out, grad_query, key_gradient, value_gradient)
```

```python
import functools

import jax
import jax.numpy as jnp
from jax import lax
from jax.experimental import pallas as pl
from jax.experimental.pallas import tpu as pltpu
from jax.sharding import Mesh, PartitionSpec as P

D = 128
G = 4
SCALE = D ** (-0.5)
LOG2E = 1.4426950408889634
C2 = SCALE * LOG2E
NEG = -1e30
PLANE = ("xl", "core", "tp")
COLS = ("xl", "core")
NT = (((1,), (1,)), ((), ()))
NN = (((1,), (0,)), ((), ()))
BF = jnp.bfloat16
F32 = jnp.float32


def dot(a, b, dims):
    return lax.dot_general(a, b, dims, preferred_element_type=F32)


def place_keys(z, own, lo1, hi1, lo2, hi2, kv_s, nz):
    for ref, offs in (
        (own, (0, -4, -8, -12)),
        (lo1, (-1, -5, -9, -13)),
        (hi1, (1, -3, -7, -11)),
        (lo2, (-6, -10)),
        (hi2, (2, -2)),
    ):
        for j, off in enumerate(offs):
            kv_s[(z + (off + nz)) % nz] = ref[j]


def chunk_mask(z, c, g, keys, rows, per):
    ki = lax.broadcasted_iota(jnp.int32, (keys, rows), 0)
    ri = lax.broadcasted_iota(jnp.int32, (keys, rows), 1)
    key_pos = (g * (keys // per) + ki // per) * rows + c * per + ki % per
    return key_pos <= z * rows + ri


def fwd_kernel(idx, qd, own, lo1, hi1, lo2, hi2, o_out, st_out, kv_s, vt_s, acc, m_s, l_s):
    z, c = idx[0], idx[1]
    rows = qd.shape[0]
    nz, per, _ = kv_s.shape
    keys = 4 * per
    place_keys(z, own, lo1, hi1, lo2, hi2, kv_s, nz)
    live = z // 4

    def flip(g, _):
        v = kv_s[pl.ds(4 * g, 4)][:, :, D:].reshape(keys, D)
        vt_s[g] = v.T
        return 0

    lax.fori_loop(0, live + 1, flip, 0)
    st_out[...] = jnp.zeros(st_out.shape, F32)
    for h in range(G):
        q = qd[:, h * D : (h + 1) * D]
        m_s[...] = jnp.full(m_s.shape, NEG, F32)
        l_s[...] = jnp.zeros(l_s.shape, F32)
        acc[...] = jnp.zeros(acc.shape, F32)

        def step(g, masked):
            k = kv_s[pl.ds(4 * g, 4)][:, :, :D].reshape(keys, D)
            s = dot(k, q, NT)
            if masked:
                s = jnp.where(chunk_mask(z, c, g, keys, rows, per), s, NEG)
            m_old = m_s[...]
            m_new = jnp.maximum(m_old, jnp.max(s, axis=0, keepdims=True))
            p = jnp.exp2((s - m_new) * C2)
            alpha = jnp.exp2((m_old - m_new) * C2)
            m_s[...] = m_new
            l_s[...] = l_s[...] * alpha + jnp.sum(p, axis=0, keepdims=True)
            acc[...] = acc[...] * alpha + dot(vt_s[g], p.astype(BF), NN)

        def full(g, _):
            step(g, False)
            return 0

        lax.fori_loop(0, live, full, 0)
        step(live, True)
        l = l_s[...]
        o_t = acc[...]
        do_t = qd[:, (G + h) * D : (G + h + 1) * D].T.astype(F32)
        st_out[pl.ds(h, 1), :] = m_s[...]
        st_out[pl.ds(G + h, 1), :] = l
        st_out[pl.ds(2 * G + h, 1), :] = jnp.sum(do_t * o_t, axis=0, keepdims=True)
        o_out[h] = o_t * (1.0 / l)


def bwd_kernel(
    idx, qd, own, lo1, hi1, lo2, hi2, o_in, st_own, st_all,
    od_out, g_own, g_lo1, g_hi1, g_lo2, g_hi2,
    kv_s, kt_s, dk_s, dv_s, dq_s,
):
    z, c = idx[0], idx[1]
    rows = qd.shape[0]
    nz, per, _ = kv_s.shape
    keys = 4 * per
    place_keys(z, own, lo1, hi1, lo2, hi2, kv_s, nz)
    live = z // 4
    dk_s[...] = jnp.zeros(dk_s.shape, F32)
    dv_s[...] = jnp.zeros(dv_s.shape, F32)

    def flip(g, _):
        kt_s[g] = kv_s[pl.ds(4 * g, 4)][:, :, :D].reshape(keys, D).T
        return 0

    lax.fori_loop(0, live + 1, flip, 0)
    for h in range(G):
        ms = [st_all[i, pl.ds(h, 1), :] for i in range(4)]
        ls = [st_all[i, pl.ds(G + h, 1), :] for i in range(4)]
        ds = [st_all[i, pl.ds(2 * G + h, 1), :] for i in range(4)]
        top = functools.reduce(jnp.maximum, ms)
        w = [jnp.exp2((m - top) * C2) for m in ms]
        total = functools.reduce(jnp.add, [a * b for a, b in zip(w, ls)])
        inv = 1.0 / total
        delta = functools.reduce(jnp.add, [a * b for a, b in zip(w, ds)]) * inv
        lse2 = top * C2 + jnp.log2(total)
        m_own = st_own[pl.ds(h, 1), :]
        l_own = st_own[pl.ds(G + h, 1), :]
        share = jnp.exp2((m_own - top) * C2) * l_own * inv
        od_out[:, h * D : (h + 1) * D] = (o_in[h] * share).T.astype(BF)
        q = qd[:, h * D : (h + 1) * D]
        do = qd[:, (G + h) * D : (G + h + 1) * D]
        dq_s[...] = jnp.zeros(dq_s.shape, F32)

        def step(g, masked):
            kv = kv_s[pl.ds(4 * g, 4)]
            k = kv[:, :, :D].reshape(keys, D)
            v = kv[:, :, D:].reshape(keys, D)
            s = dot(k, q, NT)
            p = jnp.exp2(s * C2 - lse2)
            if masked:
                p = jnp.where(chunk_mask(z, c, g, keys, rows, per), p, 0.0)
            dv_s[g] += dot(p.astype(BF), do, NN)
            dp = dot(v, do, NT)
            dsc = (p * (dp - delta)).astype(BF)
            dk_s[g] += dot(dsc, q, NN)
            dq_s[...] += dot(kt_s[g], dsc, NN)

        def full(g, _):
            step(g, False)
            return 0

        lax.fori_loop(0, live, full, 0)
        step(live, True)
        od_out[:, (G + h) * D : (G + h + 1) * D] = (dq_s[...] * SCALE).T.astype(BF)

    for ref, offs in (
        (g_own, (0, -4, -8, -12)),
        (g_lo1, (-1, -5, -9, -13)),
        (g_hi1, (1, -3, -7, -11)),
        (g_lo2, (-6, -10)),
        (g_hi2, (2, -2)),
    ):
        for j, off in enumerate(offs):
            t = (z + (off + nz)) % nz
            g, i = t // 4, t % 4
            dk = dk_s[g, pl.ds(pl.multiple_of(i * per, per), per), :] * SCALE
            dv = dv_s[g, pl.ds(pl.multiple_of(i * per, per), per), :]
            ref[j] = jnp.concatenate([dk, dv], axis=1).astype(ref.dtype)


def attention_forward(idx, qd, parts):
    rows = qd.shape[0]
    nz, per = 16, parts[0].shape[1]
    vm = pl.BlockSpec(memory_space=pltpu.VMEM)
    return pl.pallas_call(
        fwd_kernel,
        out_shape=(
            jax.ShapeDtypeStruct((G, D, rows), F32),
            jax.ShapeDtypeStruct((16, rows), F32),
        ),
        in_specs=[pl.BlockSpec(memory_space=pltpu.SMEM)] + [vm] * 6,
        out_specs=(vm, vm),
        scratch_shapes=[
            pltpu.VMEM((nz, per, 2 * D), BF),
            pltpu.VMEM((nz // 4, D, 4 * per), BF),
            pltpu.VMEM((D, rows), F32),
            pltpu.VMEM((1, rows), F32),
            pltpu.VMEM((1, rows), F32),
        ],
        compiler_params=pltpu.CompilerParams(vmem_limit_bytes=40 << 20),
        name="attn_fwd",
    )(idx, qd, *parts)


def attention_backward(idx, qd, parts, o, st, st_all):
    rows = qd.shape[0]
    nz, per = 16, parts[0].shape[1]
    vm = pl.BlockSpec(memory_space=pltpu.VMEM)
    own, lo1, hi1, lo2, hi2 = parts
    return pl.pallas_call(
        bwd_kernel,
        out_shape=(
            jax.ShapeDtypeStruct((rows, 2 * G * D), BF),
            jax.ShapeDtypeStruct(own.shape, F32),
            jax.ShapeDtypeStruct(lo1.shape, BF),
            jax.ShapeDtypeStruct(hi1.shape, BF),
            jax.ShapeDtypeStruct(lo2.shape, BF),
            jax.ShapeDtypeStruct(hi2.shape, BF),
        ),
        in_specs=[pl.BlockSpec(memory_space=pltpu.SMEM)] + [vm] * 9,
        out_specs=(vm,) * 6,
        scratch_shapes=[
            pltpu.VMEM((nz, per, 2 * D), BF),
            pltpu.VMEM((nz // 4, D, 4 * per), BF),
            pltpu.VMEM((nz // 4, 4 * per, D), F32),
            pltpu.VMEM((nz // 4, 4 * per, D), F32),
            pltpu.VMEM((D, rows), F32),
        ],
        compiler_params=pltpu.CompilerParams(vmem_limit_bytes=48 << 20),
        name="attn_bwd",
    )(idx, qd, own, lo1, hi1, lo2, hi2, o, st, st_all)


def shift(x, by):
    n = lax.axis_size("z")
    return lax.ppermute(x, "z", [(i, (i + by) % n) for i in range(n)])


def shards(query, keys, values, grad):
    tok = query.shape[0]
    tp = lax.axis_size("tp")
    cols = lax.axis_size("xl") * lax.axis_size("core")
    z = lax.axis_index("z")
    c = lax.axis_index("xl") * lax.axis_size("core") + lax.axis_index("core")
    idx = jnp.stack([z, c]).astype(jnp.int32)
    hw = G * D

    kv = jnp.concatenate([keys.reshape(tok, tp, D), values.reshape(tok, tp, D)], axis=2)
    kv = lax.all_to_all(kv.transpose(1, 0, 2), "tp", split_axis=0, concat_axis=0, tiled=True)
    kv = kv.reshape(tp * tok, 2 * D)
    qd = jnp.concatenate([query.reshape(tok, tp, hw), grad.reshape(tok, tp, hw)], axis=2)
    qd = jnp.broadcast_to(qd.transpose(1, 0, 2)[None], (cols, tp, tok, 2 * hw))
    qd = qd.reshape(cols * tp, tok, 2 * hw)
    qd = lax.all_to_all(qd, PLANE, split_axis=0, concat_axis=0, tiled=True)
    qd = qd.reshape(cols * tp * tok, 2 * hw)

    own = jnp.stack([kv, shift(kv, 4), shift(kv, 8), shift(kv, -4)])
    parts = (own, shift(own, 1), shift(own, -1), shift(own[1:3], 2), shift(own[:2], -2))

    o, st = attention_forward(idx, qd, parts)
    st_all = lax.all_gather(st, COLS, axis=0, tiled=False)
    od, g_own, g_lo1, g_hi1, g_lo2, g_hi2 = attention_backward(idx, qd, parts, o, st, st_all)

    od = lax.all_to_all(
        od.reshape(cols * tp, tok, 2 * hw), PLANE, split_axis=0, concat_axis=0, tiled=True
    )
    od = jnp.sum(od.reshape(cols, tp, tok, 2 * hw).astype(F32), axis=0).astype(BF)

    up1, down1 = shift(g_hi1, 1).astype(F32), shift(g_lo1, -1).astype(F32)
    up2, down2 = shift(g_hi2, 2).astype(F32), shift(g_lo2, -2).astype(F32)
    four = g_own + up1 + down1
    four = four + jnp.concatenate([up2, jnp.zeros_like(up2)])
    four = four + jnp.pad(down2, ((1, 1), (0, 0), (0, 0)))
    send = four[1:].astype(BF)
    gkv = four[0] + shift(send[0], -4).astype(F32)
    gkv = gkv + shift(send[1], 8).astype(F32) + shift(send[2], 4).astype(F32)
    gkv = gkv.astype(BF).reshape(tp, tok, 2 * D)
    gkv = lax.all_to_all(gkv, "tp", split_axis=0, concat_axis=0, tiled=True)

    def to_tokens(x):
        return x.transpose(1, 0, 2).reshape(tok, -1)

    return (
        to_tokens(od[:, :, :hw]),
        to_tokens(od[:, :, hw:]),
        to_tokens(gkv[:, :, :D]),
        to_tokens(gkv[:, :, D:]),
    )


def solution(mesh):
    tp = mesh.shape["tp"]
    inner = Mesh(mesh.devices.reshape(16, 2, 2, tp), ("z", "xl", "core", "tp"))
    spec = P(("z", "xl", "core", "tp"), None)
    return jax.shard_map(
        shards, mesh=inner, in_specs=(spec,) * 4, out_specs=(spec,) * 4, check_vma=False
    )
```

```python
import functools

import jax
import jax.numpy as jnp
from jax import lax
from jax.experimental import pallas as pl
from jax.experimental.pallas import tpu as pltpu
from jax.sharding import Mesh, PartitionSpec as P

D = 128
G = 4
SCALE = D ** (-0.5)
LOG2E = 1.4426950408889634
C2 = SCALE * LOG2E
NEG = -1e30
SIDE = ("xl", "tp")
COLS = ("xl", "core")
NT = (((1,), (1,)), ((), ()))
NN = (((1,), (0,)), ((), ()))
BF = jnp.bfloat16
F32 = jnp.float32


def dot(a, b, dims):
    return lax.dot_general(a, b, dims, preferred_element_type=F32)


def place_keys(z, own, lo1, hi1, lo2, hi2, kv_s, nz):
    for ref, offs in (
        (own, (0, -4, -8, -12)),
        (lo1, (-1, -5, -9, -13)),
        (hi1, (1, -3, -7, -11)),
        (lo2, (-6, -10)),
        (hi2, (2, -2)),
    ):
        for j, off in enumerate(offs):
            kv_s[(z + (off + nz)) % nz] = ref[j]


def chunk_mask(idx, g, keys, rows, per, tok):
    z, xl, core = idx[0], idx[1], idx[2]
    share = tok // 2
    k = lax.broadcasted_iota(jnp.int32, (keys, 1), 0)
    i = k % per
    src = i // share
    tp = per // tok
    key_tok = ((src // tp) * 2 + core) * per + (src % tp) * tok + xl * share + i % share
    key_pos = (g * 4 + k // per) * rows + key_tok
    r = lax.broadcasted_iota(jnp.int32, (1, rows), 1)
    half = rows // 2
    row_core = jnp.where(r < half, core, 1 - core)
    row_tok = (((r % half) // per) * 2 + row_core) * per + r % per
    return key_pos <= z * rows + row_tok


def both(a, b, lo):
    return jnp.concatenate([a[:, lo : lo + D], b[:, lo : lo + D]], axis=0)


def put_row(ref, row, x, core):
    half = x.shape[1] // 2
    ref[row : row + 1, pl.ds(pl.multiple_of(core * half, half), half)] = x[:, :half]
    ref[row : row + 1, pl.ds(pl.multiple_of((1 - core) * half, half), half)] = x[:, half:]


def get_row(ref, row, core):
    half = ref.shape[-1] // 2
    lo = ref[row : row + 1, pl.ds(pl.multiple_of(core * half, half), half)]
    hi = ref[row : row + 1, pl.ds(pl.multiple_of((1 - core) * half, half), half)]
    return jnp.concatenate([lo, hi], axis=1)


def fwd_kernel(
    tok, idx, qa, qb, own, lo1, hi1, lo2, hi2, o_out, st_out, kv_s, vt_s, acc, m_s, l_s
):
    z, core = idx[0], idx[2]
    rows = 2 * qa.shape[0]
    nz, per, _ = kv_s.shape
    keys = 4 * per
    place_keys(z, own, lo1, hi1, lo2, hi2, kv_s, nz)
    live = z // 4

    def flip(g, _):
        v = kv_s[pl.ds(4 * g, 4)][:, :, D:].reshape(keys, D)
        vt_s[g] = v.T
        return 0

    lax.fori_loop(0, live + 1, flip, 0)
    st_out[...] = jnp.zeros(st_out.shape, F32)
    for h in range(G):
        q = both(qa, qb, h * D)
        m_s[...] = jnp.full(m_s.shape, NEG, F32)
        l_s[...] = jnp.zeros(l_s.shape, F32)
        acc[...] = jnp.zeros(acc.shape, F32)

        def step(g, masked):
            k = kv_s[pl.ds(4 * g, 4)][:, :, :D].reshape(keys, D)
            s = dot(k, q, NT)
            if masked:
                s = jnp.where(chunk_mask(idx, g, keys, rows, per, tok), s, NEG)
            m_old = m_s[...]
            m_new = jnp.maximum(m_old, jnp.max(s, axis=0, keepdims=True))
            p = jnp.exp2((s - m_new) * C2)
            alpha = jnp.exp2((m_old - m_new) * C2)
            m_s[...] = m_new
            l_s[...] = l_s[...] * alpha + jnp.sum(p, axis=0, keepdims=True)
            acc[...] = acc[...] * alpha + dot(vt_s[g], p.astype(BF), NN)

        def full(g, _):
            step(g, False)
            return 0

        lax.fori_loop(0, live, full, 0)
        step(live, True)
        l = l_s[...]
        o_t = acc[...]
        do_t = both(qa, qb, (G + h) * D).T.astype(F32)
        put_row(st_out, h, m_s[...], core)
        put_row(st_out, G + h, l, core)
        put_row(st_out, 2 * G + h, jnp.sum(do_t * o_t, axis=0, keepdims=True), core)
        o_out[h] = o_t * (1.0 / l)


def bwd_kernel(
    tok, idx, qa, qb, own, lo1, hi1, lo2, hi2, o_in, st_own, st_all,
    od_a, od_b, g_own, g_lo1, g_hi1, g_lo2, g_hi2,
    kv_s, kt_s, dk_s, dv_s, dq_s,
):
    z, core = idx[0], idx[2]
    half = qa.shape[0]
    rows = 2 * half
    nz, per, _ = kv_s.shape
    keys = 4 * per
    place_keys(z, own, lo1, hi1, lo2, hi2, kv_s, nz)
    live = z // 4
    dk_s[...] = jnp.zeros(dk_s.shape, F32)
    dv_s[...] = jnp.zeros(dv_s.shape, F32)

    def flip(g, _):
        kt_s[g] = kv_s[pl.ds(4 * g, 4)][:, :, :D].reshape(keys, D).T
        return 0

    lax.fori_loop(0, live + 1, flip, 0)
    for h in range(G):
        ms = [get_row(st_all.at[i], h, core) for i in range(4)]
        ls = [get_row(st_all.at[i], G + h, core) for i in range(4)]
        ds = [get_row(st_all.at[i], 2 * G + h, core) for i in range(4)]
        top = functools.reduce(jnp.maximum, ms)
        w = [jnp.exp2((m - top) * C2) for m in ms]
        total = functools.reduce(jnp.add, [a * b for a, b in zip(w, ls)])
        inv = 1.0 / total
        delta = functools.reduce(jnp.add, [a * b for a, b in zip(w, ds)]) * inv
        lse2 = top * C2 + jnp.log2(total)
        m_own = get_row(st_own, h, core)
        l_own = get_row(st_own, G + h, core)
        share = jnp.exp2((m_own - top) * C2) * l_own * inv
        o_rows = (o_in[h] * share).T.astype(BF)
        od_a[:, h * D : (h + 1) * D] = o_rows[:half]
        od_b[:, h * D : (h + 1) * D] = o_rows[half:]
        q = both(qa, qb, h * D)
        do = both(qa, qb, (G + h) * D)
        dq_s[...] = jnp.zeros(dq_s.shape, F32)

        def step(g, masked):
            kv = kv_s[pl.ds(4 * g, 4)]
            k = kv[:, :, :D].reshape(keys, D)
            v = kv[:, :, D:].reshape(keys, D)
            s = dot(k, q, NT)
            p = jnp.exp2(s * C2 - lse2)
            if masked:
                p = jnp.where(chunk_mask(idx, g, keys, rows, per, tok), p, 0.0)
            dv_s[g] += dot(p.astype(BF), do, NN)
            dp = dot(v, do, NT)
            dsc = (p * (dp - delta)).astype(BF)
            dk_s[g] += dot(dsc, q, NN)
            dq_s[...] += dot(kt_s[g], dsc, NN)

        def full(g, _):
            step(g, False)
            return 0

        lax.fori_loop(0, live, full, 0)
        step(live, True)
        dq = (dq_s[...] * SCALE).T.astype(BF)
        od_a[:, (G + h) * D : (G + h + 1) * D] = dq[:half]
        od_b[:, (G + h) * D : (G + h + 1) * D] = dq[half:]

    for ref, offs in (
        (g_own, (0, -4, -8, -12)),
        (g_lo1, (-1, -5, -9, -13)),
        (g_hi1, (1, -3, -7, -11)),
        (g_lo2, (-6, -10)),
        (g_hi2, (2, -2)),
    ):
        for j, off in enumerate(offs):
            t = (z + (off + nz)) % nz
            g, i = t // 4, t % 4
            dk = dk_s[g, pl.ds(pl.multiple_of(i * per, per), per), :] * SCALE
            dv = dv_s[g, pl.ds(pl.multiple_of(i * per, per), per), :]
            ref[j] = jnp.concatenate([dk, dv], axis=1).astype(ref.dtype)


def attention_forward(tok, idx, qa, qb, parts):
    rows = 2 * qa.shape[0]
    nz, per = 16, parts[0].shape[1]
    vm = pl.BlockSpec(memory_space=pltpu.VMEM)
    return pl.pallas_call(
        functools.partial(fwd_kernel, tok),
        out_shape=(
            jax.ShapeDtypeStruct((G, D, rows), F32),
            jax.ShapeDtypeStruct((16, rows), F32),
        ),
        in_specs=[pl.BlockSpec(memory_space=pltpu.SMEM)] + [vm] * 7,
        out_specs=(vm, vm),
        scratch_shapes=[
            pltpu.VMEM((nz, per, 2 * D), BF),
            pltpu.VMEM((nz // 4, D, 4 * per), BF),
            pltpu.VMEM((D, rows), F32),
            pltpu.VMEM((1, rows), F32),
            pltpu.VMEM((1, rows), F32),
        ],
        compiler_params=pltpu.CompilerParams(vmem_limit_bytes=40 << 20),
        name="attn_fwd",
    )(idx, qa, qb, *parts)


def attention_backward(tok, idx, qa, qb, parts, o, st, st_all):
    nz, per = 16, parts[0].shape[1]
    vm = pl.BlockSpec(memory_space=pltpu.VMEM)
    own, lo1, hi1, lo2, hi2 = parts
    return pl.pallas_call(
        functools.partial(bwd_kernel, tok),
        out_shape=(
            jax.ShapeDtypeStruct(qa.shape, BF),
            jax.ShapeDtypeStruct(qa.shape, BF),
            jax.ShapeDtypeStruct(own.shape, F32),
            jax.ShapeDtypeStruct(lo1.shape, BF),
            jax.ShapeDtypeStruct(hi1.shape, BF),
            jax.ShapeDtypeStruct(lo2.shape, BF),
            jax.ShapeDtypeStruct(hi2.shape, BF),
        ),
        in_specs=[pl.BlockSpec(memory_space=pltpu.SMEM)] + [vm] * 10,
        out_specs=(vm,) * 7,
        scratch_shapes=[
            pltpu.VMEM((nz, per, 2 * D), BF),
            pltpu.VMEM((nz // 4, D, 4 * per), BF),
            pltpu.VMEM((nz // 4, 4 * per, D), F32),
            pltpu.VMEM((nz // 4, 4 * per, D), F32),
            pltpu.VMEM((D, 2 * qa.shape[0]), F32),
        ],
        compiler_params=pltpu.CompilerParams(vmem_limit_bytes=48 << 20),
        name="attn_bwd",
    )(idx, qa, qb, own, lo1, hi1, lo2, hi2, o, st, st_all)


def shift(x, by):
    n = lax.axis_size("z")
    return lax.ppermute(x, "z", [(i, (i + by) % n) for i in range(n)])


def other_core(x):
    return lax.ppermute(x, "core", [(0, 1), (1, 0)])


def shards(query, keys, values, grad):
    tok = query.shape[0]
    tp = lax.axis_size("tp")
    nx = lax.axis_size("xl")
    share = tok // nx
    idx = jnp.stack([lax.axis_index(a) for a in ("z", "xl", "core")]).astype(jnp.int32)
    hw = G * D

    def kv_rows(x):
        return x.reshape(nx, share, tp, D).transpose(0, 2, 1, 3)

    kv = jnp.concatenate([kv_rows(keys), kv_rows(values)], axis=2)
    qd = jnp.concatenate([query.reshape(tok, tp, hw), grad.reshape(tok, tp, hw)], axis=2)
    qd = jnp.broadcast_to(qd.transpose(1, 0, 2)[None], (nx, tp, tok, 2 * hw))
    sent = jnp.concatenate([qd, kv], axis=3).reshape(nx * tp, tok, 2 * hw + D)
    got = lax.all_to_all(sent, SIDE, split_axis=0, concat_axis=0, tiled=True)
    qa = got[:, :, : 2 * hw].reshape(nx * tp * tok, 2 * hw)
    kv = got[:, :, 2 * hw :]
    kv = jnp.concatenate([kv[:, :share], kv[:, share:]], axis=2).reshape(nx * tp * share, 2 * D)

    own = jnp.stack([kv, shift(kv, 4), shift(kv, 8), shift(kv, -4)])
    qb = other_core(qa)
    parts = (own, shift(own, 1), shift(own, -1), shift(own[1:3], 2), shift(own[:2], -2))

    o, st = attention_forward(tok, idx, qa, qb, parts)
    st_all = lax.all_gather(st, COLS, axis=0, tiled=False)
    od_a, od_b, g_own, g_lo1, g_hi1, g_lo2, g_hi2 = attention_backward(
        tok, idx, qa, qb, parts, o, st, st_all
    )

    od = od_a.astype(F32) + other_core(od_b).astype(F32)
    od = od.astype(BF).reshape(nx * tp, tok, 2 * hw)

    up1, down1 = shift(g_hi1, 1).astype(F32), shift(g_lo1, -1).astype(F32)
    up2, down2 = shift(g_hi2, 2).astype(F32), shift(g_lo2, -2).astype(F32)
    four = g_own + up1 + down1
    four = four + jnp.concatenate([up2, jnp.zeros_like(up2)])
    four = four + jnp.pad(down2, ((1, 1), (0, 0), (0, 0)))
    send = four[1:].astype(BF)
    gkv = four[0] + shift(send[0], -4).astype(F32)
    gkv = gkv + shift(send[1], 8).astype(F32) + shift(send[2], 4).astype(F32)
    gkv = gkv.astype(BF).reshape(nx * tp, share, 2 * D)
    gkv = jnp.concatenate([gkv[:, :, :D], gkv[:, :, D:]], axis=1)

    back = jnp.concatenate([od, gkv], axis=2)
    back = lax.all_to_all(back, SIDE, split_axis=0, concat_axis=0, tiled=True)
    back = back.reshape(nx, tp, tok, 2 * hw + D)
    od = jnp.sum(back[:, :, :, : 2 * hw].astype(F32), axis=0).astype(BF)

    def to_tokens(x):
        return x.transpose(1, 0, 2).reshape(tok, -1)

    def kv_tokens(x):
        return x.transpose(0, 2, 1, 3).reshape(tok, tp * D)

    return (
        to_tokens(od[:, :, :hw]),
        to_tokens(od[:, :, hw:]),
        kv_tokens(back[:, :, :share, 2 * hw :]),
        kv_tokens(back[:, :, share:, 2 * hw :]),
    )


def solution(mesh):
    tp = mesh.shape["tp"]
    inner = Mesh(mesh.devices.reshape(16, 2, 2, tp), ("z", "xl", "core", "tp"))
    spec = P(("z", "xl", "core", "tp"), None)
    return jax.shard_map(
        shards, mesh=inner, in_specs=(spec,) * 4, out_specs=(spec,) * 4, check_vma=False
    )
```

```python
import functools

import jax
import jax.numpy as jnp
from jax import lax
from jax.experimental import pallas as pl
from jax.experimental.pallas import tpu as pltpu
from jax.sharding import Mesh, PartitionSpec as P

D = 128
G = 4
SCALE = D ** (-0.5)
LOG2E = 1.4426950408889634
C2 = SCALE * LOG2E
NEG = -1e30
SIDE = ("xl", "tp")
COLS = ("xl", "core")
NT = (((1,), (1,)), ((), ()))
NN = (((1,), (0,)), ((), ()))
BF = jnp.bfloat16
F32 = jnp.float32


def dot(a, b, dims):
    return lax.dot_general(a, b, dims, preferred_element_type=F32)


PARTS = ((0, -5, 5), (-1, -6, 4), (1, -4, 6), (-2, -7, 3), (2, -3, 7), (8,))


def place_keys(z, core, parts, kv_s):
    nz = kv_s.shape[0]
    sign = 1 - 2 * core
    for ref, offs in zip(parts, PARTS):
        for j, off in enumerate(offs):
            kv_s[(z + sign * off + nz) % nz] = ref[j]


def chunk_mask(idx, g, keys, rows, per, tok):
    z, xl, core = idx[0], idx[1], idx[2]
    share = tok // 2
    k = lax.broadcasted_iota(jnp.int32, (keys, 1), 0)
    i = k % per
    src = i // share
    tp = per // tok
    key_tok = ((src // tp) * 2 + core) * per + (src % tp) * tok + xl * share + i % share
    key_pos = (g * 4 + k // per) * rows + key_tok
    r = lax.broadcasted_iota(jnp.int32, (1, rows), 1)
    half = rows // 2
    row_core = jnp.where(r < half, core, 1 - core)
    row_tok = (((r % half) // per) * 2 + row_core) * per + r % per
    return key_pos <= z * rows + row_tok


def both(a, b, lo):
    return jnp.concatenate([a[:, lo : lo + D], b[:, lo : lo + D]], axis=0)


def put_row(ref, row, x, core):
    half = x.shape[1] // 2
    ref[row : row + 1, pl.ds(pl.multiple_of(core * half, half), half)] = x[:, :half]
    ref[row : row + 1, pl.ds(pl.multiple_of((1 - core) * half, half), half)] = x[:, half:]


def get_row(ref, row, core):
    half = ref.shape[-1] // 2
    lo = ref[row : row + 1, pl.ds(pl.multiple_of(core * half, half), half)]
    hi = ref[row : row + 1, pl.ds(pl.multiple_of((1 - core) * half, half), half)]
    return jnp.concatenate([lo, hi], axis=1)


def fwd_kernel(
    tok, idx, qa, qb, p0, p1, p2, p3, p4, p5, o_out, st_out, kv_s, vt_s, acc, m_s, l_s
):
    z, core = idx[0], idx[2]
    rows = 2 * qa.shape[0]
    nz, per, _ = kv_s.shape
    keys = 4 * per
    place_keys(z, core, (p0, p1, p2, p3, p4, p5), kv_s)
    live = z // 4

    def flip(g, _):
        v = kv_s[pl.ds(4 * g, 4)][:, :, D:].reshape(keys, D)
        vt_s[g] = v.T
        return 0

    lax.fori_loop(0, live + 1, flip, 0)
    st_out[...] = jnp.zeros(st_out.shape, F32)
    for h in range(G):
        q = both(qa, qb, h * D)
        m_s[...] = jnp.full(m_s.shape, NEG, F32)
        l_s[...] = jnp.zeros(l_s.shape, F32)
        acc[...] = jnp.zeros(acc.shape, F32)

        def step(g, masked):
            k = kv_s[pl.ds(4 * g, 4)][:, :, :D].reshape(keys, D)
            s = dot(k, q, NT)
            if masked:
                s = jnp.where(chunk_mask(idx, g, keys, rows, per, tok), s, NEG)
            m_old = m_s[...]
            m_new = jnp.maximum(m_old, jnp.max(s, axis=0, keepdims=True))
            p = jnp.exp2((s - m_new) * C2)
            alpha = jnp.exp2((m_old - m_new) * C2)
            m_s[...] = m_new
            l_s[...] = l_s[...] * alpha + jnp.sum(p, axis=0, keepdims=True)
            acc[...] = acc[...] * alpha + dot(vt_s[g], p.astype(BF), NN)

        def full(g, _):
            step(g, False)
            return 0

        lax.fori_loop(0, live, full, 0)
        step(live, True)
        l = l_s[...]
        o_t = acc[...]
        do_t = both(qa, qb, (G + h) * D).T.astype(F32)
        put_row(st_out, h, m_s[...], core)
        put_row(st_out, G + h, l, core)
        put_row(st_out, 2 * G + h, jnp.sum(do_t * o_t, axis=0, keepdims=True), core)
        o_out[h] = o_t * (1.0 / l)


def bwd_kernel(
    tok, idx, qa, qb, p0, p1, p2, p3, p4, p5, o_in, st_own, st_all,
    od_a, od_b, g0, g1, g2, g3, g4, g5,
    kv_s, kt_s, dk_s, dv_s, dq_s,
):
    z, core = idx[0], idx[2]
    half = qa.shape[0]
    rows = 2 * half
    nz, per, _ = kv_s.shape
    keys = 4 * per
    place_keys(z, core, (p0, p1, p2, p3, p4, p5), kv_s)
    live = z // 4
    dk_s[...] = jnp.zeros(dk_s.shape, F32)
    dv_s[...] = jnp.zeros(dv_s.shape, F32)

    def flip(g, _):
        kt_s[g] = kv_s[pl.ds(4 * g, 4)][:, :, :D].reshape(keys, D).T
        return 0

    lax.fori_loop(0, live + 1, flip, 0)
    for h in range(G):
        ms = [get_row(st_all.at[i], h, core) for i in range(4)]
        ls = [get_row(st_all.at[i], G + h, core) for i in range(4)]
        ds = [get_row(st_all.at[i], 2 * G + h, core) for i in range(4)]
        top = functools.reduce(jnp.maximum, ms)
        w = [jnp.exp2((m - top) * C2) for m in ms]
        total = functools.reduce(jnp.add, [a * b for a, b in zip(w, ls)])
        inv = 1.0 / total
        delta = functools.reduce(jnp.add, [a * b for a, b in zip(w, ds)]) * inv
        lse2 = top * C2 + jnp.log2(total)
        m_own = get_row(st_own, h, core)
        l_own = get_row(st_own, G + h, core)
        share = jnp.exp2((m_own - top) * C2) * l_own * inv
        o_rows = (o_in[h] * share).T.astype(BF)
        od_a[:, h * D : (h + 1) * D] = o_rows[:half]
        od_b[:, h * D : (h + 1) * D] = o_rows[half:]
        q = both(qa, qb, h * D)
        do = both(qa, qb, (G + h) * D)
        dq_s[...] = jnp.zeros(dq_s.shape, F32)

        def step(g, masked):
            kv = kv_s[pl.ds(4 * g, 4)]
            k = kv[:, :, :D].reshape(keys, D)
            v = kv[:, :, D:].reshape(keys, D)
            s = dot(k, q, NT)
            p = jnp.exp2(s * C2 - lse2)
            if masked:
                p = jnp.where(chunk_mask(idx, g, keys, rows, per, tok), p, 0.0)
            dv_s[g] += dot(p.astype(BF), do, NN)
            dp = dot(v, do, NT)
            dsc = (p * (dp - delta)).astype(BF)
            dk_s[g] += dot(dsc, q, NN)
            dq_s[...] += dot(kt_s[g], dsc, NN)

        def full(g, _):
            step(g, False)
            return 0

        lax.fori_loop(0, live, full, 0)
        step(live, True)
        dq = (dq_s[...] * SCALE).T.astype(BF)
        od_a[:, (G + h) * D : (G + h + 1) * D] = dq[:half]
        od_b[:, (G + h) * D : (G + h + 1) * D] = dq[half:]

    for ref, offs in zip((g0, g1, g2, g3, g4, g5), PARTS):
        for j, off in enumerate(offs):
            t = (z + (1 - 2 * core) * off + nz) % nz
            g, i = t // 4, t % 4
            dk = dk_s[g, pl.ds(pl.multiple_of(i * per, per), per), :] * SCALE
            dv = dv_s[g, pl.ds(pl.multiple_of(i * per, per), per), :]
            ref[j] = jnp.concatenate([dk, dv], axis=1).astype(ref.dtype)


def attention_forward(tok, idx, qa, qb, parts):
    rows = 2 * qa.shape[0]
    nz, per = 16, parts[0].shape[1]
    vm = pl.BlockSpec(memory_space=pltpu.VMEM)
    return pl.pallas_call(
        functools.partial(fwd_kernel, tok),
        out_shape=(
            jax.ShapeDtypeStruct((G, D, rows), F32),
            jax.ShapeDtypeStruct((16, rows), F32),
        ),
        in_specs=[pl.BlockSpec(memory_space=pltpu.SMEM)] + [vm] * 8,
        out_specs=(vm, vm),
        scratch_shapes=[
            pltpu.VMEM((nz, per, 2 * D), BF),
            pltpu.VMEM((nz // 4, D, 4 * per), BF),
            pltpu.VMEM((D, rows), F32),
            pltpu.VMEM((1, rows), F32),
            pltpu.VMEM((1, rows), F32),
        ],
        compiler_params=pltpu.CompilerParams(vmem_limit_bytes=40 << 20),
        name="attn_fwd",
    )(idx, qa, qb, *parts)


def attention_backward(tok, idx, qa, qb, parts, o, st, st_all):
    nz, per = 16, parts[0].shape[1]
    vm = pl.BlockSpec(memory_space=pltpu.VMEM)
    return pl.pallas_call(
        functools.partial(bwd_kernel, tok),
        out_shape=(
            jax.ShapeDtypeStruct(qa.shape, BF),
            jax.ShapeDtypeStruct(qa.shape, BF),
            jax.ShapeDtypeStruct(parts[0].shape, F32),
            *(jax.ShapeDtypeStruct(p.shape, BF) for p in parts[1:]),
        ),
        in_specs=[pl.BlockSpec(memory_space=pltpu.SMEM)] + [vm] * 11,
        out_specs=(vm,) * 8,
        scratch_shapes=[
            pltpu.VMEM((nz, per, 2 * D), BF),
            pltpu.VMEM((nz // 4, D, 4 * per), BF),
            pltpu.VMEM((nz // 4, 4 * per, D), F32),
            pltpu.VMEM((nz // 4, 4 * per, D), F32),
            pltpu.VMEM((D, 2 * qa.shape[0]), F32),
        ],
        compiler_params=pltpu.CompilerParams(vmem_limit_bytes=48 << 20),
        name="attn_bwd",
    )(idx, qa, qb, *parts, o, st, st_all)


def shift(x, by):
    n = lax.axis_size("z")
    route = [(2 * i + c, 2 * ((i + by * (1 - 2 * c)) % n) + c) for i in range(n) for c in range(2)]
    return lax.ppermute(x, ("z", "core"), route)


def other_core(x):
    return lax.ppermute(x, "core", [(0, 1), (1, 0)])


def shards(query, keys, values, grad):
    tok = query.shape[0]
    tp = lax.axis_size("tp")
    nx = lax.axis_size("xl")
    share = tok // nx
    idx = jnp.stack([lax.axis_index(a) for a in ("z", "xl", "core")]).astype(jnp.int32)
    hw = G * D

    def kv_rows(x):
        return x.reshape(nx, share, tp, D).transpose(0, 2, 1, 3)

    kv = jnp.concatenate([kv_rows(keys), kv_rows(values)], axis=2)
    qd = jnp.concatenate([query.reshape(tok, tp, hw), grad.reshape(tok, tp, hw)], axis=2)
    qd = jnp.broadcast_to(qd.transpose(1, 0, 2)[None], (nx, tp, tok, 2 * hw))
    sent = jnp.concatenate([qd, kv], axis=3).reshape(nx * tp, tok, 2 * hw + D)
    got = lax.all_to_all(sent, SIDE, split_axis=0, concat_axis=0, tiled=True)
    qa = got[:, :, : 2 * hw].reshape(nx * tp * tok, 2 * hw)
    kv = got[:, :, 2 * hw :]
    kv = jnp.concatenate([kv[:, :share], kv[:, share:]], axis=2).reshape(nx * tp * share, 2 * D)

    own = jnp.stack([kv, shift(kv, 5), shift(kv, -5)])
    qb = other_core(qa)
    parts = (own, *(shift(own, by) for by in (1, -1, 2, -2)), shift(own[2:], -3))

    o, st = attention_forward(tok, idx, qa, qb, parts)
    st_all = lax.all_gather(st, COLS, axis=0, tiled=False)
    od_a, od_b, g_own, *g_far = attention_backward(
        tok, idx, qa, qb, parts, o, st, st_all
    )

    od = od_a.astype(F32) + other_core(od_b).astype(F32)
    od = od.astype(BF).reshape(nx * tp, tok, 2 * hw)

    three = g_own
    for g, by in zip(g_far[:4], (-1, 1, -2, 2)):
        three = three + shift(g, by).astype(F32)
    last = three[2] + shift(g_far[4], 3)[0].astype(F32)
    gkv = three[0] + shift(three[1].astype(BF), -5).astype(F32)
    gkv = gkv + shift(last.astype(BF), 5).astype(F32)
    gkv = gkv.astype(BF).reshape(nx * tp, share, 2 * D)
    gkv = jnp.concatenate([gkv[:, :, :D], gkv[:, :, D:]], axis=1)

    back = jnp.concatenate([od, gkv], axis=2)
    back = lax.all_to_all(back, SIDE, split_axis=0, concat_axis=0, tiled=True)
    back = back.reshape(nx, tp, tok, 2 * hw + D)
    od = jnp.sum(back[:, :, :, : 2 * hw].astype(F32), axis=0).astype(BF)

    def to_tokens(x):
        return x.transpose(1, 0, 2).reshape(tok, -1)

    def kv_tokens(x):
        return x.transpose(0, 2, 1, 3).reshape(tok, tp * D)

    return (
        to_tokens(od[:, :, :hw]),
        to_tokens(od[:, :, hw:]),
        kv_tokens(back[:, :, :share, 2 * hw :]),
        kv_tokens(back[:, :, share:, 2 * hw :]),
    )


def solution(mesh):
    tp = mesh.shape["tp"]
    inner = Mesh(mesh.devices.reshape(16, 2, 2, tp), ("z", "xl", "core", "tp"))
    spec = P(("z", "xl", "core", "tp"), None)
    return jax.shard_map(
        shards, mesh=inner, in_specs=(spec,) * 4, out_specs=(spec,) * 4, check_vma=False
    )
```

```python
import functools

import jax
import jax.numpy as jnp
from jax import lax
from jax.experimental import pallas as pl
from jax.experimental.pallas import tpu as pltpu
from jax.sharding import Mesh, PartitionSpec as P

D = 128
G = 4
SCALE = D ** (-0.5)
LOG2E = 1.4426950408889634
C2 = SCALE * LOG2E
NEG = -1e30
SIDE = ("xl", "tp")
COLS = ("xl", "core")
NT = (((1,), (1,)), ((), ()))
NN = (((1,), (0,)), ((), ()))
BF = jnp.bfloat16
F32 = jnp.float32

EVEN = (0, 4, 2, 6)
ODD = (1, 5, 3, 7)


def dot(a, b, dims):
    return lax.dot_general(a, b, dims, preferred_element_type=F32)


def is_live(z, core, k, planes):
    return jnp.where(core == 0, k <= z, k >= planes - z)


def distance(order, j):
    k = jnp.int32(order[0])
    for i in range(1, len(order)):
        k = jnp.where(j == i, order[i], k)
    return k


def own_mask(idx, per, rows, tok):
    xl, core = idx[1], idx[2]
    share = tok // 2
    k = lax.broadcasted_iota(jnp.int32, (per, 1), 0)
    src = k // share
    tp = per // tok
    key_tok = ((src // tp) * 2 + core) * per + (src % tp) * tok + xl * share + k % share
    r = lax.broadcasted_iota(jnp.int32, (1, rows), 1)
    half = rows // 2
    row_core = jnp.where(r < half, core, 1 - core)
    row_tok = (((r % half) // per) * 2 + row_core) * per + r % per
    return key_tok <= row_tok


def both(a, b, lo):
    return jnp.concatenate([a[:, lo : lo + D], b[:, lo : lo + D]], axis=0)


def put_row(ref, row, x, core):
    half = x.shape[1] // 2
    ref[row : row + 1, pl.ds(pl.multiple_of(core * half, half), half)] = x[:, :half]
    ref[row : row + 1, pl.ds(pl.multiple_of((1 - core) * half, half), half)] = x[:, half:]


def get_row(ref, row, core):
    half = ref.shape[-1] // 2
    lo = ref[row : row + 1, pl.ds(pl.multiple_of(core * half, half), half)]
    hi = ref[row : row + 1, pl.ds(pl.multiple_of((1 - core) * half, half), half)]
    return jnp.concatenate([lo, hi], axis=1)


def attend(qa, qb, kv, ml, acc, mask=None):
    k, vt = kv[:, :D], kv[:, D:].T
    for h in range(G):
        s = dot(k, both(qa, qb, h * D), NT)
        if mask is not None:
            s = jnp.where(mask, s, NEG)
        m_old = ml[h : h + 1, :]
        m_new = jnp.maximum(m_old, jnp.max(s, axis=0, keepdims=True))
        p = jnp.exp2((s - m_new) * C2)
        alpha = jnp.exp2((m_old - m_new) * C2)
        ml[h : h + 1, :] = m_new
        ml[G + h : G + h + 1, :] = ml[G + h : G + h + 1, :] * alpha + jnp.sum(
            p, axis=0, keepdims=True
        )
        acc[h] = acc[h] * alpha + dot(vt, p.astype(BF), NN)


def attend_planes(idx, planes, order, first, qa, qb, kvs, ml, acc):
    z, core = idx[0], idx[2]
    per = kvs.shape[1]

    def plane(j, _):
        @pl.when(is_live(z, core, distance(order, j), planes))
        def _():
            kv = kvs[pl.ds(2 * j, 2)].reshape(2 * per, 2 * D)
            attend(qa, qb, kv, ml, acc)

        return 0

    lax.fori_loop(first, len(order), plane, 0)


def fwd_even_kernel(planes, tok, idx, qa, qb, kvs, ml, acc):
    rows = 2 * qa.shape[0]
    ml[0:G, :] = jnp.full((G, rows), NEG, F32)
    ml[G:, :] = jnp.zeros((ml.shape[0] - G, rows), F32)
    acc[...] = jnp.zeros(acc.shape, F32)
    attend(qa, qb, kvs[0], ml, acc, own_mask(idx, kvs.shape[1], rows, tok))
    attend_planes(idx, planes, EVEN, 1, qa, qb, kvs, ml, acc)


def fwd_odd_kernel(planes, idx, qa, qb, kvs, kv8, ml_in, acc_in, o_out, st_out, ml, acc):
    z, core = idx[0], idx[2]
    ml[...] = ml_in[...]
    acc[...] = acc_in[...]
    attend_planes(idx, planes, ODD, 0, qa, qb, kvs, ml, acc)

    @pl.when(is_live(z, core, planes // 2, planes))
    def _():
        attend(qa, qb, kv8[...], ml, acc)

    st_out[...] = jnp.zeros(st_out.shape, F32)
    for h in range(G):
        o_t = acc[h]
        l = ml[G + h : G + h + 1, :]
        do_t = both(qa, qb, (G + h) * D).T.astype(F32)
        put_row(st_out, h, ml[h : h + 1, :], core)
        put_row(st_out, G + h, l, core)
        put_row(st_out, 2 * G + h, jnp.sum(do_t * o_t, axis=0, keepdims=True), core)
        o_out[h] = o_t * (1.0 / l)


def joined_stats(st_all, core, h):
    ms = [get_row(st_all.at[i], h, core) for i in range(4)]
    ls = [get_row(st_all.at[i], G + h, core) for i in range(4)]
    ds = [get_row(st_all.at[i], 2 * G + h, core) for i in range(4)]
    top = functools.reduce(jnp.maximum, ms)
    w = [jnp.exp2((m - top) * C2) for m in ms]
    total = functools.reduce(jnp.add, [a * b for a, b in zip(w, ls)])
    inv = 1.0 / total
    delta = functools.reduce(jnp.add, [a * b for a, b in zip(w, ds)]) * inv
    return top, inv, top * C2 + jnp.log2(total), delta


def store_stats(st_all, core, rows_s):
    for h in range(G):
        _, _, lse2, delta = joined_stats(st_all, core, h)
        rows_s[h : h + 1, :] = lse2
        rows_s[G + h : G + h + 1, :] = delta


def grads(qa, qb, kv, rows_s, dq, mask=None):
    k, v = kv[:, :D], kv[:, D:]
    kt = k.T
    dk = jnp.zeros(k.shape, F32)
    dv = jnp.zeros(k.shape, F32)
    for h in range(G):
        q, do = both(qa, qb, h * D), both(qa, qb, (G + h) * D)
        s = dot(k, q, NT)
        p = jnp.exp2(s * C2 - rows_s[h : h + 1, :])
        if mask is not None:
            p = jnp.where(mask, p, 0.0)
        dv = dv + dot(p.astype(BF), do, NN)
        dp = dot(v, do, NT)
        ds = (p * (dp - rows_s[G + h : G + h + 1, :])).astype(BF)
        dk = dk + dot(ds, q, NN)
        dq[h] += dot(kt, ds, NN)
    return jnp.concatenate([dk * SCALE, dv], axis=1)


def grad_planes(idx, planes, order, first, qa, qb, kvs, rows_s, dq, g_out):
    z, core = idx[0], idx[2]
    per = kvs.shape[1]

    def plane(j, _):
        live = is_live(z, core, distance(order, j), planes)

        @pl.when(live)
        def _():
            kv = kvs[pl.ds(2 * j, 2)].reshape(2 * per, 2 * D)
            g = grads(qa, qb, kv, rows_s, dq)
            g_out[pl.ds(2 * j, 2)] = g.reshape(2, per, 2 * D).astype(g_out.dtype)

        @pl.when(jnp.logical_not(live))
        def _():
            g_out[pl.ds(2 * j, 2)] = jnp.zeros((2, per, 2 * D), g_out.dtype)

        return 0

    lax.fori_loop(first, len(order), plane, 0)


def bwd_odd_kernel(planes, idx, qa, qb, kvs, kv8, st_all, g_out, g8_out, dq, rows_s):
    z, core = idx[0], idx[2]
    store_stats(st_all, core, rows_s)
    dq[...] = jnp.zeros(dq.shape, F32)
    grad_planes(idx, planes, ODD, 0, qa, qb, kvs, rows_s, dq, g_out)
    live = is_live(z, core, planes // 2, planes)

    @pl.when(live)
    def _():
        g8_out[...] = grads(qa, qb, kv8[...], rows_s, dq).astype(g8_out.dtype)

    @pl.when(jnp.logical_not(live))
    def _():
        g8_out[...] = jnp.zeros(g8_out.shape, g8_out.dtype)


def bwd_even_kernel(
    planes, tok, idx, qa, qb, kvs, st_own, st_all, o_in, dq_in, g_out, od_a, od_b, dq, rows_s
):
    core = idx[2]
    half = qa.shape[0]
    store_stats(st_all, core, rows_s)
    dq[...] = dq_in[...]
    mask = own_mask(idx, kvs.shape[1], 2 * half, tok)
    g_out[0] = grads(qa, qb, kvs[0], rows_s, dq, mask)
    g_out[1] = jnp.zeros(kvs.shape[1:], F32)
    grad_planes(idx, planes, EVEN, 1, qa, qb, kvs, rows_s, dq, g_out)
    for h in range(G):
        top, inv, _, _ = joined_stats(st_all, core, h)
        m_own = get_row(st_own, h, core)
        l_own = get_row(st_own, G + h, core)
        share = jnp.exp2((m_own - top) * C2) * l_own * inv
        o = (o_in[h] * share).T.astype(BF)
        g = (dq[h] * SCALE).T.astype(BF)
        for ref, lo in ((od_a, 0), (od_b, half)):
            ref[:, h * D : (h + 1) * D] = o[lo : lo + half]
            ref[:, (G + h) * D : (G + h + 1) * D] = g[lo : lo + half]


def call(kernel, name, out_shape, args, scratch=()):
    vm = pl.BlockSpec(memory_space=pltpu.VMEM)
    return pl.pallas_call(
        kernel,
        out_shape=tuple(jax.ShapeDtypeStruct(s, d) for s, d in out_shape),
        in_specs=[pl.BlockSpec(memory_space=pltpu.SMEM)] + [vm] * (len(args) - 1),
        out_specs=(vm,) * len(out_shape),
        scratch_shapes=[pltpu.VMEM(s, F32) for s in scratch],
        compiler_params=pltpu.CompilerParams(vmem_limit_bytes=40 << 20),
        name=name,
    )(*args)


def shift(x, by):
    n = lax.axis_size("z")
    route = [(2 * i + c, 2 * ((i + by * (1 - 2 * c)) % n) + c) for i in range(n) for c in range(2)]
    return lax.ppermute(x, ("z", "core"), route)


def other_core(x):
    return lax.ppermute(x, "core", [(0, 1), (1, 0)])


def shards(query, keys, values, grad):
    tok = query.shape[0]
    tp = lax.axis_size("tp")
    nx = lax.axis_size("xl")
    planes = lax.axis_size("z")
    share = tok // nx
    rows = 2 * nx * tp * tok
    idx = jnp.stack([lax.axis_index(a) for a in ("z", "xl", "core")]).astype(jnp.int32)
    hw = G * D

    def kv_rows(x):
        return x.reshape(nx, share, tp, D).transpose(0, 2, 1, 3)

    kv = jnp.concatenate([kv_rows(keys), kv_rows(values)], axis=2)
    qd = jnp.concatenate([query.reshape(tok, tp, hw), grad.reshape(tok, tp, hw)], axis=2)
    qd = jnp.broadcast_to(qd.transpose(1, 0, 2)[None], (nx, tp, tok, 2 * hw))
    sent = jnp.concatenate([qd, kv], axis=3).reshape(nx * tp, tok, 2 * hw + D)
    got = lax.all_to_all(sent, SIDE, split_axis=0, concat_axis=0, tiled=True)
    qa = got[:, :, : 2 * hw].reshape(nx * tp * tok, 2 * hw)
    kv = got[:, :, 2 * hw :]
    kv = jnp.concatenate([kv[:, :share], kv[:, share:]], axis=2).reshape(nx * tp * share, 2 * D)

    at0 = jnp.stack([kv, other_core(kv)])
    at4 = shift(at0, 4)
    qb = other_core(qa)
    at04 = jnp.concatenate([at0, at4])
    even = jnp.concatenate([at04, shift(at04, 2)])
    odd = shift(even, 1)
    at8 = shift(even[6], 2)

    heads = ((G, D, rows), F32)
    ml, acc = call(
        functools.partial(fwd_even_kernel, planes, tok),
        "fwd_even",
        (((2 * G, rows), F32), heads),
        (idx, qa, qb, even),
    )
    o, st = call(
        functools.partial(fwd_odd_kernel, planes),
        "fwd_odd",
        (heads, ((16, rows), F32)),
        (idx, qa, qb, odd, at8, ml, acc),
        ((2 * G, rows), (G, D, rows)),
    )
    st_all = lax.all_gather(st, COLS, axis=0, tiled=False)
    g_odd, g8, dq = call(
        functools.partial(bwd_odd_kernel, planes),
        "bwd_odd",
        ((odd.shape, BF), (at8.shape, BF), heads),
        (idx, qa, qb, odd, at8, st_all),
        ((2 * G, rows),),
    )
    near, near8 = shift(g_odd, -1), shift(g8, -2)
    g_even, od_a, od_b = call(
        functools.partial(bwd_even_kernel, planes, tok),
        "bwd_even",
        ((even.shape, F32), (qa.shape, BF), (qa.shape, BF)),
        (idx, qa, qb, even, st, st_all, o, dq),
        ((G, D, rows), (2 * G, rows)),
    )
    od = od_a.astype(F32) + other_core(od_b).astype(F32)
    od = od.astype(BF).reshape(nx * tp, tok, 2 * hw)

    g_even = g_even + near.astype(F32)
    g26 = jnp.concatenate([g_even[4:6], g_even[6:7] + near8[None].astype(F32), g_even[7:]])
    g04 = g_even[:4] + shift(g26.astype(BF), -2).astype(F32)
    g0 = g04[:2] + shift(g04[2:].astype(BF), -4).astype(F32)
    gkv = g0[0] + other_core(g0[1].astype(BF)).astype(F32)
    gkv = gkv.astype(BF).reshape(nx * tp, share, 2 * D)
    gkv = jnp.concatenate([gkv[:, :, :D], gkv[:, :, D:]], axis=1)

    back = jnp.concatenate([od, gkv], axis=2)
    back = lax.all_to_all(back, SIDE, split_axis=0, concat_axis=0, tiled=True)
    back = back.reshape(nx, tp, tok, 2 * hw + D)
    od = jnp.sum(back[:, :, :, : 2 * hw].astype(F32), axis=0).astype(BF)

    def to_tokens(x):
        return x.transpose(1, 0, 2).reshape(tok, -1)

    def kv_tokens(x):
        return x.transpose(0, 2, 1, 3).reshape(tok, tp * D)

    return (
        to_tokens(od[:, :, :hw]),
        to_tokens(od[:, :, hw:]),
        kv_tokens(back[:, :, :share, 2 * hw :]),
        kv_tokens(back[:, :, share:, 2 * hw :]),
    )


def solution(mesh):
    tp = mesh.shape["tp"]
    inner = Mesh(mesh.devices.reshape(16, 2, 2, tp), ("z", "xl", "core", "tp"))
    spec = P(("z", "xl", "core", "tp"), None)
    return jax.shard_map(
        shards, mesh=inner, in_specs=(spec,) * 4, out_specs=(spec,) * 4, check_vma=False
    )
```

```python
import functools

import jax
import jax.numpy as jnp
from jax import lax
from jax.experimental import pallas as pl
from jax.experimental.pallas import tpu as pltpu
from jax.sharding import Mesh, PartitionSpec as P

D = 128
G = 4
SCALE = D ** (-0.5)
LOG2E = 1.4426950408889634
C2 = SCALE * LOG2E
NEG = -1e30
DEAD = 2e30
SIDE = ("xl", "tp")
COLS = ("xl", "core")
NT = (((1,), (1,)), ((), ()))
NN = (((1,), (0,)), ((), ()))
BF = jnp.bfloat16
F32 = jnp.float32

EVEN = (0, 4, 2, 6)
ODD = (1, 5, 3, 7)


def dot(a, b, dims):
    return lax.dot_general(a, b, dims, preferred_element_type=F32)


def is_live(z, core, k, planes):
    return jnp.where(core == 0, k <= z, k >= planes - z)


def distance(order, j):
    k = jnp.int32(order[0])
    for i in range(1, len(order)):
        k = jnp.where(j == i, order[i], k)
    return k


def own_mask(idx, per, rows, tok):
    xl, core = idx[1], idx[2]
    share = tok // 2
    k = lax.broadcasted_iota(jnp.int32, (per, 1), 0)
    src = k // share
    tp = per // tok
    key_tok = ((src // tp) * 2 + core) * per + (src % tp) * tok + xl * share + k % share
    r = lax.broadcasted_iota(jnp.int32, (1, rows), 1)
    half = rows // 2
    row_core = jnp.where(r < half, core, 1 - core)
    row_tok = (((r % half) // per) * 2 + row_core) * per + r % per
    return key_tok <= row_tok


def both(a, b, lo):
    return jnp.concatenate([a[:, lo : lo + D], b[:, lo : lo + D]], axis=0)


def put_row(ref, row, x, core):
    half = x.shape[1] // 2
    ref[row : row + 1, pl.ds(pl.multiple_of(core * half, half), half)] = x[:, :half]
    ref[row : row + 1, pl.ds(pl.multiple_of((1 - core) * half, half), half)] = x[:, half:]


def get_row(ref, row, core):
    half = ref.shape[-1] // 2
    lo = ref[row : row + 1, pl.ds(pl.multiple_of(core * half, half), half)]
    hi = ref[row : row + 1, pl.ds(pl.multiple_of((1 - core) * half, half), half)]
    return jnp.concatenate([lo, hi], axis=1)


def gate(z, core, k, planes):
    return jnp.where(is_live(z, core, k, planes), 0.0, DEAD).astype(F32)


def attend(qa, qb, kv, spans, ml, acc):
    k, vt = kv[:, :D], kv[:, D:].T
    ahead = dot(k, both(qa, qb, 0), NT)
    for h in range(G):
        s = ahead
        if h + 1 < G:
            ahead = dot(k, both(qa, qb, (h + 1) * D), NT)
        m_old = ml[h : h + 1, :]
        m_new, at, cuts = m_old, 0, []
        for size, shut, mask in spans:
            cut = s[at : at + size]
            if mask is not None:
                cut = jnp.where(mask, cut, NEG)
            top = jnp.max(cut, axis=0, keepdims=True)
            m_new = jnp.maximum(m_new, top if shut is None else top - shut)
            cuts.append(cut)
            at += size
        total, ps = jnp.zeros_like(m_old), []
        for cut, (_, shut, _) in zip(cuts, spans):
            p = jnp.exp2((cut - (m_new if shut is None else m_new + shut)) * C2)
            total = total + jnp.sum(p, axis=0, keepdims=True)
            ps.append(p.astype(BF))
        alpha = jnp.exp2((m_old - m_new) * C2)
        ml[h : h + 1, :] = m_new
        ml[G + h : G + h + 1, :] = ml[G + h : G + h + 1, :] * alpha + total
        acc[h] = acc[h] * alpha + dot(vt, jnp.concatenate(ps, axis=0), NN)


def fwd_even_kernel(planes, tok, idx, qa, qb, kvs, ml, acc):
    z, core = idx[0], idx[2]
    rows = 2 * qa.shape[0]
    per = kvs.shape[1]
    shut = [gate(z, core, k, planes) for k in EVEN]
    ml[0:G, :] = jnp.full((G, rows), NEG, F32)
    ml[G:, :] = jnp.zeros((ml.shape[0] - G, rows), F32)
    acc[...] = jnp.zeros(acc.shape, F32)
    kv = jnp.concatenate([kvs[0], kvs[2], kvs[3]], axis=0)
    spans = ((per, None, own_mask(idx, per, rows, tok)), (2 * per, shut[1], None))
    attend(qa, qb, kv, spans, ml, acc)

    @pl.when(shut[2] + shut[3] < 2 * DEAD)
    def _():
        kv = kvs[4:].reshape(4 * per, 2 * D)
        attend(qa, qb, kv, [(2 * per, s, None) for s in shut[2:]], ml, acc)


def fwd_odd_kernel(planes, idx, qa, qb, kvs, kv8, ml_in, acc_in, o_out, st_out, ml, acc):
    z, core = idx[0], idx[2]
    per = kvs.shape[1]
    ml[...] = ml_in[...]
    acc[...] = acc_in[...]

    def pair(j, _):
        shut = [gate(z, core, distance(ODD[i::2], j), planes) for i in range(2)]

        @pl.when(shut[0] + shut[1] < 2 * DEAD)
        def _():
            kv = kvs[pl.ds(4 * j, 4)].reshape(4 * per, 2 * D)
            attend(qa, qb, kv, [(2 * per, s, None) for s in shut], ml, acc)

        return 0

    lax.fori_loop(0, 2, pair, 0)

    @pl.when(is_live(z, core, planes // 2, planes))
    def _():
        attend(qa, qb, kv8[...], [(per, None, None)], ml, acc)

    st_out[...] = jnp.zeros(st_out.shape, F32)
    for h in range(G):
        o_t = acc[h]
        l = ml[G + h : G + h + 1, :]
        do_t = both(qa, qb, (G + h) * D).T.astype(F32)
        put_row(st_out, h, ml[h : h + 1, :], core)
        put_row(st_out, G + h, l, core)
        put_row(st_out, 2 * G + h, jnp.sum(do_t * o_t, axis=0, keepdims=True), core)
        o_out[h] = o_t * (1.0 / l)


def joined_stats(st_all, core, h):
    ms = [get_row(st_all.at[i], h, core) for i in range(4)]
    ls = [get_row(st_all.at[i], G + h, core) for i in range(4)]
    ds = [get_row(st_all.at[i], 2 * G + h, core) for i in range(4)]
    top = functools.reduce(jnp.maximum, ms)
    w = [jnp.exp2((m - top) * C2) for m in ms]
    total = functools.reduce(jnp.add, [a * b for a, b in zip(w, ls)])
    inv = 1.0 / total
    delta = functools.reduce(jnp.add, [a * b for a, b in zip(w, ds)]) * inv
    return top, inv, top * C2 + jnp.log2(total), delta


def store_stats(st_all, core, rows_s):
    for h in range(G):
        _, _, lse2, delta = joined_stats(st_all, core, h)
        rows_s[h : h + 1, :] = lse2
        rows_s[G + h : G + h + 1, :] = delta


def grads(qa, qb, kv, spans, rows_s, dq):
    k, v = kv[:, :D], kv[:, D:]
    kt = k.T
    dk = jnp.zeros(k.shape, F32)
    dv = jnp.zeros(k.shape, F32)

    def products(h):
        return dot(k, both(qa, qb, h * D), NT), dot(v, both(qa, qb, (G + h) * D), NT)

    ahead = products(0)
    for h in range(G):
        s, dp = ahead
        if h + 1 < G:
            ahead = products(h + 1)
        lse2, delta = rows_s[h : h + 1, :], rows_s[G + h : G + h + 1, :]
        ps, dss, at = [], [], 0
        for size, shut, mask in spans:
            p = jnp.exp2(s[at : at + size] * C2 - (lse2 if shut is None else lse2 + shut))
            if mask is not None:
                p = jnp.where(mask, p, 0.0)
            ps.append(p.astype(BF))
            dss.append((p * (dp[at : at + size] - delta)).astype(BF))
            at += size
        ds = jnp.concatenate(dss, axis=0)
        dv = dv + dot(jnp.concatenate(ps, axis=0), both(qa, qb, (G + h) * D), NN)
        dk = dk + dot(ds, both(qa, qb, h * D), NN)
        dq[h] += dot(kt, ds, NN)
    return jnp.concatenate([dk * SCALE, dv], axis=1)


def grad_pair(qa, qb, kvs, at, shut, rows_s, dq, g_out):
    per = kvs.shape[1]
    live = shut[0] + shut[1] < 2 * DEAD

    @pl.when(live)
    def _():
        kv = kvs[pl.ds(at, 4)].reshape(4 * per, 2 * D)
        g = grads(qa, qb, kv, [(2 * per, s, None) for s in shut], rows_s, dq)
        g_out[pl.ds(at, 4)] = g.reshape(4, per, 2 * D).astype(g_out.dtype)

    @pl.when(jnp.logical_not(live))
    def _():
        g_out[pl.ds(at, 4)] = jnp.zeros((4, per, 2 * D), g_out.dtype)


def bwd_odd_kernel(planes, idx, qa, qb, kvs, kv8, st_all, g_out, g8_out, dq, rows_s):
    z, core = idx[0], idx[2]
    store_stats(st_all, core, rows_s)
    dq[...] = jnp.zeros(dq.shape, F32)

    def pair(j, _):
        shut = [gate(z, core, distance(ODD[i::2], j), planes) for i in range(2)]
        grad_pair(qa, qb, kvs, 4 * j, shut, rows_s, dq, g_out)
        return 0

    lax.fori_loop(0, 2, pair, 0)
    live = is_live(z, core, planes // 2, planes)

    @pl.when(live)
    def _():
        spans = [(kv8.shape[0], None, None)]
        g8_out[...] = grads(qa, qb, kv8[...], spans, rows_s, dq).astype(g8_out.dtype)

    @pl.when(jnp.logical_not(live))
    def _():
        g8_out[...] = jnp.zeros(g8_out.shape, g8_out.dtype)


def bwd_26_kernel(planes, idx, qa, qb, kvs, st_all, dq_in, g_out, dq, rows_s):
    z, core = idx[0], idx[2]
    store_stats(st_all, core, rows_s)
    dq[...] = dq_in[...]
    shut = [gate(z, core, k, planes) for k in EVEN[2:]]
    grad_pair(qa, qb, kvs, 0, shut, rows_s, dq, g_out)


def bwd_04_kernel(
    planes, tok, idx, qa, qb, kvs, st_own, st_all, o_in, dq_in, near, g_out, od_a, od_b, dq, rows_s
):
    z, core = idx[0], idx[2]
    half = qa.shape[0]
    per = kvs.shape[1]
    store_stats(st_all, core, rows_s)
    dq[...] = dq_in[...]
    mask = own_mask(idx, per, 2 * half, tok)
    spans = ((per, None, mask), (2 * per, gate(z, core, EVEN[1], planes), None))
    kv = jnp.concatenate([kvs[0], kvs[2], kvs[3]], axis=0)
    g = grads(qa, qb, kv, spans, rows_s, dq)
    g_out[0] = g[:per] + near[0].astype(F32)
    g_out[1] = near[1].astype(F32)
    g_out[2] = g[per : 2 * per] + near[2].astype(F32)
    g_out[3] = g[2 * per :] + near[3].astype(F32)
    for h in range(G):
        top, inv, _, _ = joined_stats(st_all, core, h)
        m_own = get_row(st_own, h, core)
        l_own = get_row(st_own, G + h, core)
        share = jnp.exp2((m_own - top) * C2) * l_own * inv
        o = (o_in[h] * share).T.astype(BF)
        g = (dq[h] * SCALE).T.astype(BF)
        for ref, lo in ((od_a, 0), (od_b, half)):
            ref[:, h * D : (h + 1) * D] = o[lo : lo + half]
            ref[:, (G + h) * D : (G + h + 1) * D] = g[lo : lo + half]


def call(kernel, name, out_shape, args, scratch=()):
    vm = pl.BlockSpec(memory_space=pltpu.VMEM)
    return pl.pallas_call(
        kernel,
        out_shape=tuple(jax.ShapeDtypeStruct(s, d) for s, d in out_shape),
        in_specs=[pl.BlockSpec(memory_space=pltpu.SMEM)] + [vm] * (len(args) - 1),
        out_specs=(vm,) * len(out_shape),
        scratch_shapes=[pltpu.VMEM(s, F32) for s in scratch],
        compiler_params=pltpu.CompilerParams(vmem_limit_bytes=44 << 20),
        name=name,
    )(*args)


def shift(x, by):
    n = lax.axis_size("z")
    route = [(2 * i + c, 2 * ((i + by * (1 - 2 * c)) % n) + c) for i in range(n) for c in range(2)]
    return lax.ppermute(x, ("z", "core"), route)


def other_core(x):
    return lax.ppermute(x, "core", [(0, 1), (1, 0)])


def shards(query, keys, values, grad):
    tok = query.shape[0]
    tp = lax.axis_size("tp")
    nx = lax.axis_size("xl")
    planes = lax.axis_size("z")
    share = tok // nx
    rows = 2 * nx * tp * tok
    idx = jnp.stack([lax.axis_index(a) for a in ("z", "xl", "core")]).astype(jnp.int32)
    hw = G * D

    def kv_rows(x):
        return x.reshape(nx, share, tp, D).transpose(0, 2, 1, 3)

    kv = jnp.concatenate([kv_rows(keys), kv_rows(values)], axis=2)
    qd = jnp.concatenate([query.reshape(tok, tp, hw), grad.reshape(tok, tp, hw)], axis=2)
    qd = jnp.broadcast_to(qd.transpose(1, 0, 2)[None], (nx, tp, tok, 2 * hw))
    sent = jnp.concatenate([qd, kv], axis=3).reshape(nx * tp, tok, 2 * hw + D)
    got = lax.all_to_all(sent, SIDE, split_axis=0, concat_axis=0, tiled=True)
    qa = got[:, :, : 2 * hw].reshape(nx * tp * tok, 2 * hw)
    kv = got[:, :, 2 * hw :]
    kv = jnp.concatenate([kv[:, :share], kv[:, share:]], axis=2).reshape(nx * tp * share, 2 * D)

    at0 = jnp.stack([kv, other_core(kv)])
    at4 = shift(at0, 4)
    qb = other_core(qa)
    at04 = jnp.concatenate([at0, at4])
    even = jnp.concatenate([at04, shift(at04, 2)])
    odd = shift(even, 1)
    at8 = shift(even[6], 2)

    heads = ((G, D, rows), F32)
    ml, acc = call(
        functools.partial(fwd_even_kernel, planes, tok),
        "fwd_even",
        (((2 * G, rows), F32), heads),
        (idx, qa, qb, even),
    )
    o, st = call(
        functools.partial(fwd_odd_kernel, planes),
        "fwd_odd",
        (heads, ((16, rows), F32)),
        (idx, qa, qb, odd, at8, ml, acc),
        ((2 * G, rows), (G, D, rows)),
    )
    st_all = lax.all_gather(st, COLS, axis=0, tiled=False)
    g_odd, g8, dq = call(
        functools.partial(bwd_odd_kernel, planes),
        "bwd_odd",
        ((odd.shape, BF), (at8.shape, BF), heads),
        (idx, qa, qb, odd, at8, st_all),
        ((2 * G, rows),),
    )
    near, near8 = shift(g_odd, -1), shift(g8, -2)
    g_26, dq = call(
        functools.partial(bwd_26_kernel, planes),
        "bwd_26",
        ((even[4:].shape, F32), heads),
        (idx, qa, qb, even[4:], st_all, dq),
        ((2 * G, rows),),
    )
    g_04, od_a, od_b = call(
        functools.partial(bwd_04_kernel, planes, tok),
        "bwd_04",
        ((at04.shape, F32), (qa.shape, BF), (qa.shape, BF)),
        (idx, qa, qb, at04, st, st_all, o, dq, near[:4]),
        ((G, D, rows), (2 * G, rows)),
    )
    od = od_a.astype(F32) + other_core(od_b).astype(F32)
    od = od.astype(BF).reshape(nx * tp, tok, 2 * hw)

    g_26 = g_26 + near[4:].astype(F32)
    g_26 = jnp.concatenate([g_26[:2], g_26[2:3] + near8[None].astype(F32), g_26[3:]])
    g04 = g_04 + shift(g_26.astype(BF), -2).astype(F32)
    g0 = g04[:2] + shift(g04[2:].astype(BF), -4).astype(F32)
    gkv = g0[0] + other_core(g0[1].astype(BF)).astype(F32)
    gkv = gkv.astype(BF).reshape(nx * tp, share, 2 * D)
    gkv = jnp.concatenate([gkv[:, :, :D], gkv[:, :, D:]], axis=1)

    back = jnp.concatenate([od, gkv], axis=2)
    back = lax.all_to_all(back, SIDE, split_axis=0, concat_axis=0, tiled=True)
    back = back.reshape(nx, tp, tok, 2 * hw + D)
    od = jnp.sum(back[:, :, :, : 2 * hw].astype(F32), axis=0).astype(BF)

    def to_tokens(x):
        return x.transpose(1, 0, 2).reshape(tok, -1)

    def kv_tokens(x):
        return x.transpose(0, 2, 1, 3).reshape(tok, tp * D)

    return (
        to_tokens(od[:, :, :hw]),
        to_tokens(od[:, :, hw:]),
        kv_tokens(back[:, :, :share, 2 * hw :]),
        kv_tokens(back[:, :, share:, 2 * hw :]),
    )


def solution(mesh):
    tp = mesh.shape["tp"]
    inner = Mesh(mesh.devices.reshape(16, 2, 2, tp), ("z", "xl", "core", "tp"))
    spec = P(("z", "xl", "core", "tp"), None)
    return jax.shard_map(
        shards, mesh=inner, in_specs=(spec,) * 4, out_specs=(spec,) * 4, check_vma=False
    )
```

```python
import functools

import jax
import jax.numpy as jnp
from jax import lax
from jax.experimental import pallas as pl
from jax.experimental.pallas import tpu as pltpu
from jax.sharding import Mesh, PartitionSpec as P

D = 128
G = 4
SCALE = D ** (-0.5)
LOG2E = 1.4426950408889634
C2 = SCALE * LOG2E
NEG = -1e30
DEAD = 2e30
SIDE = ("xl", "tp")
COLS = ("xl", "core")
NT = (((1,), (1,)), ((), ()))
NN = (((1,), (0,)), ((), ()))
BF = jnp.bfloat16
F32 = jnp.float32

EVEN = (0, 4, 2, 6)
ODD = (1, 5, 3, 7)


def dot(a, b, dims):
    return lax.dot_general(a, b, dims, preferred_element_type=F32)


def is_live(z, core, k, planes):
    return jnp.where(core == 0, k <= z, k >= planes - z)


def own_mask(idx, per, rows, tok):
    xl, core = idx[1], idx[2]
    share = tok // 2
    k = lax.broadcasted_iota(jnp.int32, (per, 1), 0)
    src = k // share
    tp = per // tok
    key_tok = ((src // tp) * 2 + core) * per + (src % tp) * tok + xl * share + k % share
    r = lax.broadcasted_iota(jnp.int32, (1, rows), 1)
    half = rows // 2
    row_core = jnp.where(r < half, core, 1 - core)
    row_tok = (((r % half) // per) * 2 + row_core) * per + r % per
    return key_tok <= row_tok


def both(a, b, lo):
    return jnp.concatenate([a[:, lo : lo + D], b[:, lo : lo + D]], axis=0)


def put_row(ref, row, x, core):
    half = x.shape[1] // 2
    ref[row : row + 1, pl.ds(pl.multiple_of(core * half, half), half)] = x[:, :half]
    ref[row : row + 1, pl.ds(pl.multiple_of((1 - core) * half, half), half)] = x[:, half:]


def get_row(ref, row, core):
    half = ref.shape[-1] // 2
    lo = ref[row : row + 1, pl.ds(pl.multiple_of(core * half, half), half)]
    hi = ref[row : row + 1, pl.ds(pl.multiple_of((1 - core) * half, half), half)]
    return jnp.concatenate([lo, hi], axis=1)


def gates(idx, planes, order):
    live = [is_live(idx[0], idx[2], k, planes) for k in order]
    return [jnp.where(x, 0.0, DEAD).astype(F32) for x in live], functools.reduce(jnp.logical_or, live)


def attend(qa, qb, kv, spans, ml, acc):
    k, vt = kv[:, :D], kv[:, D:].T
    ahead = dot(k, both(qa, qb, 0), NT)
    for h in range(G):
        s = ahead
        if h + 1 < G:
            ahead = dot(k, both(qa, qb, (h + 1) * D), NT)
        m_old = ml[h : h + 1, :]
        m_new, at, cuts = m_old, 0, []
        for size, shut, mask in spans:
            cut = s[at : at + size]
            if mask is not None:
                cut = jnp.where(mask, cut, NEG)
            top = jnp.max(cut, axis=0, keepdims=True)
            m_new = jnp.maximum(m_new, top if shut is None else top - shut)
            cuts.append(cut)
            at += size
        total, ps = jnp.zeros_like(m_old), []
        for cut, (_, shut, _) in zip(cuts, spans):
            p = jnp.exp2((cut - (m_new if shut is None else m_new + shut)) * C2)
            total = total + jnp.sum(p, axis=0, keepdims=True)
            ps.append(p.astype(BF))
        alpha = jnp.exp2((m_old - m_new) * C2)
        ml[h : h + 1, :] = m_new
        ml[G + h : G + h + 1, :] = ml[G + h : G + h + 1, :] * alpha + total
        acc[h] = acc[h] * alpha + dot(vt, jnp.concatenate(ps, axis=0), NN)


def fwd_even_kernel(planes, tok, idx, qa, qb, mine, other, ml, acc):
    rows = 2 * qa.shape[0]
    per = mine.shape[1]
    shut, live = gates(idx, planes, EVEN[1:])
    spans = [(per, s, None) for s in shut]
    ml[0:G, :] = jnp.full((G, rows), NEG, F32)
    ml[G:, :] = jnp.zeros((ml.shape[0] - G, rows), F32)
    acc[...] = jnp.zeros(acc.shape, F32)
    own = (per, None, own_mask(idx, per, rows, tok))
    attend(qa, qb, mine[...].reshape(-1, 2 * D), [own] + spans, ml, acc)

    @pl.when(live)
    def _():
        attend(qa, qb, other[1:].reshape(-1, 2 * D), spans, ml, acc)


def fwd_odd_kernel(planes, idx, qa, qb, mine, other, kv8, ml_in, acc_in, o_out, st_out, ml, acc):
    core = idx[2]
    per = mine.shape[1]
    ml[...] = ml_in[...]
    acc[...] = acc_in[...]
    shut, live = gates(idx, planes, ODD)
    shut8, live8 = gates(idx, planes, (planes // 2,))
    spans = [(per, s, None) for s in shut]

    @pl.when(live)
    def _():
        attend(qa, qb, other[...].reshape(-1, 2 * D), spans, ml, acc)

    @pl.when(jnp.logical_or(live, live8))
    def _():
        kv = jnp.concatenate([mine[...].reshape(-1, 2 * D), kv8[...]], axis=0)
        attend(qa, qb, kv, spans + [(per, shut8[0], None)], ml, acc)

    st_out[...] = jnp.zeros(st_out.shape, F32)
    for h in range(G):
        o_t = acc[h]
        l = ml[G + h : G + h + 1, :]
        do_t = both(qa, qb, (G + h) * D).T.astype(F32)
        put_row(st_out, h, ml[h : h + 1, :], core)
        put_row(st_out, G + h, l, core)
        put_row(st_out, 2 * G + h, jnp.sum(do_t * o_t, axis=0, keepdims=True), core)
        o_out[h] = o_t * (1.0 / l)


def joined_stats(st_all, core, h):
    ms = [get_row(st_all.at[i], h, core) for i in range(4)]
    ls = [get_row(st_all.at[i], G + h, core) for i in range(4)]
    ds = [get_row(st_all.at[i], 2 * G + h, core) for i in range(4)]
    top = functools.reduce(jnp.maximum, ms)
    w = [jnp.exp2((m - top) * C2) for m in ms]
    total = functools.reduce(jnp.add, [a * b for a, b in zip(w, ls)])
    inv = 1.0 / total
    delta = functools.reduce(jnp.add, [a * b for a, b in zip(w, ds)]) * inv
    return top, inv, top * C2 + jnp.log2(total), delta


def store_stats(st_all, core, rows_s):
    for h in range(G):
        _, _, lse2, delta = joined_stats(st_all, core, h)
        rows_s[h : h + 1, :] = lse2
        rows_s[G + h : G + h + 1, :] = delta


def grads(qa, qb, kv, spans, rows_s, dq):
    k, v = kv[:, :D], kv[:, D:]
    kt = k.T
    dk = jnp.zeros(k.shape, F32)
    dv = jnp.zeros(k.shape, F32)

    def products(h):
        return dot(k, both(qa, qb, h * D), NT), dot(v, both(qa, qb, (G + h) * D), NT)

    ahead = products(0)
    for h in range(G):
        s, dp = ahead
        if h + 1 < G:
            ahead = products(h + 1)
        lse2, delta = rows_s[h : h + 1, :], rows_s[G + h : G + h + 1, :]
        ps, dss, at = [], [], 0
        for size, shut, mask in spans:
            p = jnp.exp2(s[at : at + size] * C2 - (lse2 if shut is None else lse2 + shut))
            if mask is not None:
                p = jnp.where(mask, p, 0.0)
            ps.append(p.astype(BF))
            dss.append((p * (dp[at : at + size] - delta)).astype(BF))
            at += size
        ds = jnp.concatenate(dss, axis=0)
        dv = dv + dot(jnp.concatenate(ps, axis=0), both(qa, qb, (G + h) * D), NN)
        dk = dk + dot(ds, both(qa, qb, h * D), NN)
        dq[h] += dot(kt, ds, NN)
    return jnp.concatenate([dk * SCALE, dv], axis=1)


def zero_all(refs):
    for ref in refs:
        ref[...] = jnp.zeros(ref.shape, ref.dtype)


def bwd_odd_other_kernel(planes, idx, qa, qb, other, st_all, g_out, dq, rows_s):
    per = other.shape[1]
    store_stats(st_all, idx[2], rows_s)
    dq[...] = jnp.zeros(dq.shape, F32)
    shut, live = gates(idx, planes, ODD)

    @pl.when(live)
    def _():
        spans = [(per, s, None) for s in shut]
        g = grads(qa, qb, other[...].reshape(-1, 2 * D), spans, rows_s, dq)
        g_out[...] = g.reshape(g_out.shape).astype(g_out.dtype)

    @pl.when(jnp.logical_not(live))
    def _():
        zero_all((g_out,))


def bwd_odd_mine_kernel(planes, idx, qa, qb, mine, kv8, st_all, dq_in, g_out, g8_out, dq, rows_s):
    per = mine.shape[1]
    store_stats(st_all, idx[2], rows_s)
    dq[...] = dq_in[...]
    shut, live = gates(idx, planes, ODD + (planes // 2,))

    @pl.when(live)
    def _():
        spans = [(per, s, None) for s in shut]
        kv = jnp.concatenate([mine[...].reshape(-1, 2 * D), kv8[...]], axis=0)
        g = grads(qa, qb, kv, spans, rows_s, dq)
        g_out[...] = g[: 4 * per].reshape(g_out.shape).astype(g_out.dtype)
        g8_out[...] = g[4 * per :].astype(g8_out.dtype)

    @pl.when(jnp.logical_not(live))
    def _():
        zero_all((g_out, g8_out))


def bwd_even_other_kernel(planes, idx, qa, qb, other, st_all, dq_in, g_out, dq, rows_s):
    per = other.shape[1]
    store_stats(st_all, idx[2], rows_s)
    dq[...] = dq_in[...]
    shut, live = gates(idx, planes, EVEN[1:])

    @pl.when(live)
    def _():
        spans = [(per, s, None) for s in shut]
        g = grads(qa, qb, other[1:].reshape(-1, 2 * D), spans, rows_s, dq)
        g_out[...] = g.reshape(g_out.shape)

    @pl.when(jnp.logical_not(live))
    def _():
        zero_all((g_out,))


def bwd_even_mine_kernel(
    planes, tok, idx, qa, qb, mine, st_own, st_all, o_in, dq_in, g_out, od_a, od_b, dq, rows_s
):
    core = idx[2]
    half = qa.shape[0]
    per = mine.shape[1]
    store_stats(st_all, core, rows_s)
    dq[...] = dq_in[...]
    shut, _ = gates(idx, planes, EVEN[1:])
    spans = [(per, None, own_mask(idx, per, 2 * half, tok))] + [(per, s, None) for s in shut]
    g = grads(qa, qb, mine[...].reshape(-1, 2 * D), spans, rows_s, dq)
    g_out[...] = g.reshape(g_out.shape)
    for h in range(G):
        top, inv, _, _ = joined_stats(st_all, core, h)
        m_own = get_row(st_own, h, core)
        l_own = get_row(st_own, G + h, core)
        share = jnp.exp2((m_own - top) * C2) * l_own * inv
        o = (o_in[h] * share).T.astype(BF)
        g = (dq[h] * SCALE).T.astype(BF)
        for ref, lo in ((od_a, 0), (od_b, half)):
            ref[:, h * D : (h + 1) * D] = o[lo : lo + half]
            ref[:, (G + h) * D : (G + h + 1) * D] = g[lo : lo + half]


def call(kernel, name, out_shape, args, scratch=()):
    vm = pl.BlockSpec(memory_space=pltpu.VMEM)
    return pl.pallas_call(
        kernel,
        out_shape=tuple(jax.ShapeDtypeStruct(s, d) for s, d in out_shape),
        in_specs=[pl.BlockSpec(memory_space=pltpu.SMEM)] + [vm] * (len(args) - 1),
        out_specs=(vm,) * len(out_shape),
        scratch_shapes=[pltpu.VMEM(s, F32) for s in scratch],
        compiler_params=pltpu.CompilerParams(vmem_limit_bytes=44 << 20),
        name=name,
    )(*args)


def shift(x, by):
    n = lax.axis_size("z")
    route = [(2 * i + c, 2 * ((i + by * (1 - 2 * c)) % n) + c) for i in range(n) for c in range(2)]
    return lax.ppermute(x, ("z", "core"), route)


def other_core(x):
    return lax.ppermute(x, "core", [(0, 1), (1, 0)])


def shards(query, keys, values, grad):
    tok = query.shape[0]
    tp = lax.axis_size("tp")
    nx = lax.axis_size("xl")
    planes = lax.axis_size("z")
    share = tok // nx
    rows = 2 * nx * tp * tok
    idx = jnp.stack([lax.axis_index(a) for a in ("z", "xl", "core")]).astype(jnp.int32)
    hw = G * D

    def kv_rows(x):
        return x.reshape(nx, share, tp, D).transpose(0, 2, 1, 3)

    kv = jnp.concatenate([kv_rows(keys), kv_rows(values)], axis=2)
    qd = jnp.concatenate([query.reshape(tok, tp, hw), grad.reshape(tok, tp, hw)], axis=2)
    qd = jnp.broadcast_to(qd.transpose(1, 0, 2)[None], (nx, tp, tok, 2 * hw))
    sent = jnp.concatenate([qd, kv], axis=3).reshape(nx * tp, tok, 2 * hw + D)
    got = lax.all_to_all(sent, SIDE, split_axis=0, concat_axis=0, tiled=True)
    qa = got[:, :, : 2 * hw].reshape(nx * tp * tok, 2 * hw)
    kv = got[:, :, 2 * hw :]
    kv = jnp.concatenate([kv[:, :share], kv[:, share:]], axis=2).reshape(nx * tp * share, 2 * D)

    def gathered(x):
        at04 = jnp.stack([x, shift(x, 4)])
        even = jnp.concatenate([at04, shift(at04, 2)])
        return even, shift(even, 1)

    even_m, odd_m = gathered(kv)
    even_o, odd_o = gathered(other_core(kv))
    at8 = shift(even_m[3], 2)
    qb = other_core(qa)

    heads = ((G, D, rows), F32)
    blocks = even_m.shape
    ml, acc = call(
        functools.partial(fwd_even_kernel, planes, tok),
        "fwd_even",
        (((2 * G, rows), F32), heads),
        (idx, qa, qb, even_m, even_o),
    )
    o, st = call(
        functools.partial(fwd_odd_kernel, planes),
        "fwd_odd",
        (heads, ((16, rows), F32)),
        (idx, qa, qb, odd_m, odd_o, at8, ml, acc),
        ((2 * G, rows), (G, D, rows)),
    )
    st_all = lax.all_gather(st, COLS, axis=0, tiled=False)
    g_odd_o, dq = call(
        functools.partial(bwd_odd_other_kernel, planes),
        "bwd_odd_o",
        ((blocks, BF), heads),
        (idx, qa, qb, odd_o, st_all),
        ((2 * G, rows),),
    )
    near_o = shift(g_odd_o, -1).astype(F32)
    g_odd_m, g8, dq = call(
        functools.partial(bwd_odd_mine_kernel, planes),
        "bwd_odd_m",
        ((blocks, BF), (at8.shape, BF), heads),
        (idx, qa, qb, odd_m, at8, st_all, dq),
        ((2 * G, rows),),
    )
    near_m, near8 = shift(g_odd_m, -1).astype(F32), shift(g8, -2).astype(F32)
    g_o, dq = call(
        functools.partial(bwd_even_other_kernel, planes),
        "bwd_even_o",
        (((3, *blocks[1:]), F32), heads),
        (idx, qa, qb, even_o, st_all, dq),
        ((2 * G, rows),),
    )
    far_o = shift((g_o[1:] + near_o[2:]).astype(BF), -2).astype(F32)
    g_m, od_a, od_b = call(
        functools.partial(bwd_even_mine_kernel, planes, tok),
        "bwd_even_m",
        ((blocks, F32), (qa.shape, BF), (qa.shape, BF)),
        (idx, qa, qb, even_m, st, st_all, o, dq),
        ((G, D, rows), (2 * G, rows)),
    )
    od = od_a.astype(F32) + other_core(od_b).astype(F32)
    od = od.astype(BF).reshape(nx * tp, tok, 2 * hw)

    g_m = g_m + near_m
    far_m = jnp.stack([g_m[2], g_m[3] + near8]).astype(BF)
    far_m = shift(far_m, -2).astype(F32)
    last_o = shift((g_o[0] + near_o[1] + far_o[1]).astype(BF), -4).astype(F32)
    last_m = shift((g_m[1] + far_m[1]).astype(BF), -4).astype(F32)
    gkv_o = other_core((near_o[0] + far_o[0] + last_o).astype(BF)).astype(F32)
    gkv = g_m[0] + far_m[0] + last_m + gkv_o
    gkv = gkv.astype(BF).reshape(nx * tp, share, 2 * D)
    gkv = jnp.concatenate([gkv[:, :, :D], gkv[:, :, D:]], axis=1)

    back = jnp.concatenate([od, gkv], axis=2)
    back = lax.all_to_all(back, SIDE, split_axis=0, concat_axis=0, tiled=True)
    back = back.reshape(nx, tp, tok, 2 * hw + D)
    od = jnp.sum(back[:, :, :, : 2 * hw].astype(F32), axis=0).astype(BF)

    def to_tokens(x):
        return x.transpose(1, 0, 2).reshape(tok, -1)

    def kv_tokens(x):
        return x.transpose(0, 2, 1, 3).reshape(tok, tp * D)

    return (
        to_tokens(od[:, :, :hw]),
        to_tokens(od[:, :, hw:]),
        kv_tokens(back[:, :, :share, 2 * hw :]),
        kv_tokens(back[:, :, share:, 2 * hw :]),
    )


def solution(mesh):
    tp = mesh.shape["tp"]
    inner = Mesh(mesh.devices.reshape(16, 2, 2, tp), ("z", "xl", "core", "tp"))
    spec = P(("z", "xl", "core", "tp"), None)
    return jax.shard_map(
        shards, mesh=inner, in_specs=(spec,) * 4, out_specs=(spec,) * 4, check_vma=False
    )
```
